512 devices in a mesh: shot: 32 (over y_hi, z, core), slab: 16 (over x, y_lo).
Axes of the slice: x: 4, y: 8 (y_hi: 2, y_lo: 4; y = y_hi * 4 + y_lo), z: 8, core: 2. Of those that a mesh axis runs over, the one named last changes fastest.
Arguments:
- previous_field: bfloat16 [32, 128, 32, 128], P('shot', 'slab'), may hold values from -6 to 6
- current_field: bfloat16 [32, 128, 32, 128], P('shot', 'slab'), may hold values from -6 to 6
- adjoint_next: bfloat16 [32, 128, 32, 128], P('shot', 'slab'), may hold values from -6 to 6
- adjoint_current: bfloat16 [32, 128, 32, 128], P('shot', 'slab'), may hold values from -6 to 6
- velocity: float32 [128, 32, 128], P('slab'), may hold values from 1.5 to 4.2
- wavelet: float32 [32, 6], P('shot'), may hold values from -24 to 24
- source_cell: int32 [32], P('shot'), may hold values from 0 to 524287
- receiver_cell: int32 [32, 256], P('shot'), may hold values from 0 to 524287
- observed: float32 [32, 6, 256], P('shot'), may hold values from -6 to 6
- weight_in: bfloat16 [27, 2, 64], replicated, may hold values from -0.875 to 0.875
- bias_in: float32 [64], replicated, may hold values from -3 to 3
- weight_mid: bfloat16 [27, 64, 64], replicated, may hold values from -0.15625 to 0.15625
- bias_mid: float32 [64], replicated, may hold values from -3 to 3
- weight_out: bfloat16 [27, 64, 1], replicated, may hold values from -0.15625 to 0.15625
- bias_out: float32 [1], replicated, may hold values from -3 to 3
Outputs:
- velocity_next: float32 [128, 32, 128], P('slab')
- misfit: float32 [32, 6, 256], P('shot')
The draws below stay inside these ranges and needn't reach their ends.
All inputs are finite; a program needn't handle non-finite values.
Results may differ from the reference program's by a relative error of at most 0.0023.
Values may be sent and summed in bfloat16 or wider, within the bound.
A program may use at most 64 MiB of HBM per device.

```python
import jax
import jax.numpy as jnp
from jax import lax

NY = 32
NZ = 128
FWD = 6
REC = 256
C = 64
SHOTS = 32
NX = 128


def touch_ends(values, key, smallest, high):
    spot = [jax.random.randint(jax.random.fold_in(key, axis), (), 0, length) for axis, length in enumerate(values.shape)]
    longest = values.shape.index(max(values.shape))
    beside = spot[:longest] + [(spot[longest] + 1) % values.shape[longest]] + spot[longest + 1:]
    return values.at[tuple(spot)].set(smallest).at[tuple(beside)].set(high)


def block_levels(rng, extent, cuts, smallest, largest):
    def one(dim, parts):
        steps = jax.random.uniform(jax.random.fold_in(jax.random.fold_in(rng, 6), dim), (parts,), jnp.float32, smallest / len(cuts), largest / len(cuts))
        return jnp.repeat(jnp.exp(steps), extent[dim] // parts).reshape((-1,) + (1,) * (len(extent) - dim - 1))

    loudness = one(*cuts[0])
    for cut in cuts[1:]:
        loudness = loudness * one(*cut)
    return loudness


def bell_draw(own_key, dims, width, bound, cuts=(), kind=jnp.bfloat16):
    gain = block_levels(own_key, dims, cuts, -0.22, 0.18) if cuts else 1.0
    array = jax.random.normal(own_key, dims, jnp.float32) * width * gain
    return jnp.minimum(jnp.maximum(array, -bound), bound).astype(kind)


def setup_inputs(seed: int = 0) -> dict:
    streams_of = jax.random.split(jax.random.key(seed), 16)
    previous_field = bell_draw(streams_of[0], (SHOTS, NX, NY, NZ), 1.0, 6.0, ((0, 32), (1, 16)))
    current_field = bell_draw(streams_of[1], (SHOTS, NX, NY, NZ), 1.0, 6.0, ((0, 32), (1, 16)))
    adjoint_next = bell_draw(streams_of[2], (SHOTS, NX, NY, NZ), 1.0, 6.0, ((0, 32), (1, 16)))
    adjoint_current = bell_draw(streams_of[3], (SHOTS, NX, NY, NZ), 1.0, 6.0, ((0, 32), (1, 16)))
    velocity = jnp.clip(1.5 + 2.6999998 * jax.random.uniform(streams_of[4], (NX, NY, NZ), jnp.float32) ** block_levels(streams_of[4], (NX, NY, NZ), ((0, 16),), -0.2, 0.2), 1.5, 4.2)
    wavelet = bell_draw(streams_of[5], (SHOTS, FWD), 4.0, 24.0, ((0, 32),), jnp.float32)
    source_cell = touch_ends(jax.random.randint(streams_of[6], (SHOTS,), 0, NX * NY * NZ), jax.random.fold_in(streams_of[6], 1), 0, (NX * NY * NZ) - 1).astype(jnp.int32)
    receiver_cell = touch_ends(jax.random.randint(streams_of[7], (SHOTS, REC), 0, NX * NY * NZ), jax.random.fold_in(streams_of[7], 1), 0, (NX * NY * NZ) - 1).astype(jnp.int32)
    observed = bell_draw(streams_of[8], (SHOTS, FWD, REC), 1.0, 6.0, ((0, 32),), jnp.float32)
    weight_in = bell_draw(streams_of[9], (27, 2, C), 54 ** -0.5, 0.875)
    bias_in = bell_draw(streams_of[10], (C,), 0.5, 3.0, (), jnp.float32)
    weight_mid = bell_draw(streams_of[11], (27, C, C), (27 * C) ** -0.5, 0.15625)
    bias_mid = bell_draw(streams_of[12], (C,), 0.5, 3.0, (), jnp.float32)
    weight_out = bell_draw(streams_of[13], (27, C, 1), (27 * C) ** -0.5, 0.15625)
    bias_out = bell_draw(streams_of[14], (1,), 0.5, 3.0, (), jnp.float32)
    return dict(previous_field=previous_field, current_field=current_field, adjoint_next=adjoint_next, adjoint_current=adjoint_current, velocity=velocity, wavelet=wavelet, source_cell=source_cell, receiver_cell=receiver_cell, observed=observed, weight_in=weight_in, bias_in=bias_in, weight_mid=weight_mid, bias_mid=bias_mid, weight_out=weight_out, bias_out=bias_out)


coeffs = (-205.0 / 72.0, 8.0 / 5.0, -1.0 / 5.0, 8.0 / 315.0, -1.0 / 560.0)
courant = 0.1
learn_rate = 0.2
center_speed = 3.0


def laplace(widened):
    count_rows = widened.shape[0] - 8
    middle = widened[4:4 + count_rows]
    width_y = middle.shape[1]
    width_z = middle.shape[2]
    padded = jnp.pad(middle, ((0, 0), (4, 4), (4, 4)))
    accumulated = (3.0 * coeffs[0]) * middle
    for offset in range(1, 5):
        summed = widened[4 + offset:4 + offset + count_rows] + widened[4 - offset:4 - offset + count_rows]
        summed = summed + padded[:, 4 + offset:4 + offset + width_y, 4:4 + width_z] + padded[:, 4 - offset:4 - offset + width_y, 4:4 + width_z]
        summed = summed + padded[:, 4:4 + width_y, 4 + offset:4 + offset + width_z] + padded[:, 4:4 + width_y, 4 - offset:4 - offset + width_z]
        accumulated = accumulated + coeffs[offset] * summed
    return accumulated


def full_laplace(wavefield):
    return laplace(jnp.pad(wavefield, ((4, 4), (0, 0), (0, 0))))


def evolve(kappa, previous, current, later, adjoint_now, pulses, source_one, receivers, observed_row):
    previous = previous.astype(jnp.float32)
    current = current.astype(jnp.float32)
    later = later.astype(jnp.float32)
    adjoint_now = adjoint_now.astype(jnp.float32)
    snapshots = []
    recorded = []
    for moment in range(FWD):
        laplacian = full_laplace(current)
        advanced = 2.0 * current - previous + kappa * laplacian
        advanced = advanced.reshape(-1).at[source_one].add(pulses[moment]).reshape(current.shape)
        recorded.append(advanced.reshape(-1)[receivers])
        snapshots.append(laplacian)
        previous, current = current, advanced
    misfit_rows = jnp.stack(recorded) - observed_row
    imaging = jnp.zeros(current.shape, jnp.float32)
    for moment in reversed(range(FWD)):
        laplacian = full_laplace(adjoint_now)
        advanced = 2.0 * adjoint_now - later + kappa * laplacian
        advanced = advanced.reshape(-1).at[receivers].add(misfit_rows[moment]).reshape(current.shape)
        imaging = imaging + advanced * snapshots[moment]
        later, adjoint_now = adjoint_now, advanced
    return imaging, misfit_rows


def convolve(features, weight, shift):
    kernel = weight.astype(jnp.float32).reshape(3, 3, 3, weight.shape[1], weight.shape[2])
    result = lax.conv_general_dilated(features.astype(jnp.float32)[None], kernel, (1, 1, 1), "SAME", dimension_numbers=("NCDHW", "DHWIO", "NCDHW"), precision=lax.Precision.HIGHEST)[0]
    return result + shift[:, None, None, None]


def reference(previous_field, current_field, adjoint_next, adjoint_current, velocity, wavelet, source_cell, receiver_cell, observed, weight_in, bias_in, weight_mid, bias_mid, weight_out, bias_out):
    scaled = velocity * courant
    kappa = scaled * scaled

    def one_shot(carried, inputs):
        previous, current, later, adjoint_now, pulses, source_one, receivers, observed_row = inputs
        imaging, misfit_rows = evolve(kappa, previous, current, later, adjoint_now, pulses, source_one, receivers, observed_row)
        return carried + imaging, misfit_rows

    start_sum = jnp.zeros(velocity.shape, jnp.float32)
    image_sum, misfit = lax.scan(one_shot, start_sum, (previous_field, current_field, adjoint_next, adjoint_current, wavelet, source_cell, receiver_cell, observed))
    mean_image = image_sum / SHOTS
    update = learn_rate * mean_image
    moved = velocity - update
    features = jnp.stack([moved - center_speed, update]).astype(jnp.bfloat16)
    hidden_one = jnp.maximum(convolve(features, weight_in, bias_in), 0.0).astype(jnp.bfloat16)
    hidden_two = jnp.maximum(convolve(hidden_one, weight_mid, bias_mid), 0.0).astype(jnp.bfloat16)
    velocity_next = moved + convolve(hidden_two, weight_out, bias_out)[0]
    return velocity_next, misfit
```

```python
import functools

import jax
import jax.numpy as jnp
from jax import lax
from jax.experimental import pallas as pl
from jax.experimental.pallas import tpu as pltpu
from jax.sharding import PartitionSpec as P

COEFFS = (-205.0 / 72.0, 8.0 / 5.0, -1.0 / 5.0, 8.0 / 315.0, -1.0 / 560.0)
COURANT = 0.1
RATE = 0.2
CENTER = 3.0
MID = 2.75
MESH = pl.DeviceIdType.MESH
F32 = jnp.float32
BF16 = jnp.bfloat16
NT = (((1,), (1,)), ((), ()))
STEPS = 6
TOP, ROWS = 8, 32
YS = slice(TOP, TOP + ROWS)


def dot(a, b):
    return jnp.dot(a, b, preferred_element_type=F32)


def split(x, pieces):
    parts = []
    for _ in range(pieces):
        part = x.astype(BF16)
        parts.append(part)
        x = x - part.astype(F32)
    return parts


def z_combine(g, lane):
    low = jnp.where(lane == 0, 0.0, pltpu.roll(g[0:64], 1, 1))
    high = jnp.where(lane == 127, 0.0, pltpu.roll(g[128:192], 127, 1))
    return g[64:128] + low + high


def kernel(
    slabs, shots,
    prev, cur, anext, acur, vel, wav, src, rec, obs, w1, b1, wm, b2, w3, b3,
    out, mis,
    u0, u1, wa0, wa1, da, db, zs, js, kap, lap, hom, img, imgt,
    sv, rv, rc, rp, sb, rb, tr, rt, mf, hot, pick, lane_hot, src_hot, bands, bandl,
    ri, fs, rf, feat, g1, h1, h2, row, ro,
    init_s, init_r, round_s, round_r, tr_s, tr_r, im_s, im_r, ft_s, ft_r, ou_s, ou_r,
):
    s = lax.axis_index("shot")
    b = lax.axis_index("slab")

    def shot_at(k):
        return lax.rem(s + k + shots, shots)

    def slab_at(k):
        return lax.rem(b + k + slabs, slabs)

    def inside(k):
        return jnp.where((b + k >= 0) & (b + k < slabs), 1.0, 0.0).astype(F32)

    def send(source, target, ss, rs, shot, slab):
        copy = pltpu.make_async_remote_copy(
            src_ref=source, dst_ref=target, send_sem=ss, recv_sem=rs,
            device_id=(shot, slab), device_id_type=MESH)
        copy.start()
        return copy

    barrier = pltpu.get_barrier_semaphore()
    peers = [(s, slab_at(k)) for k in range(1, slabs)]
    peers += [(shot_at(k), b) for k in range(1, shots)]
    cross = [(dx, dy) for dy in range(-3, 4) for dx in (-1, 0, 1) if (dx, dy) != (0, 0)]
    peers += [(shot_at(dy), slab_at(dx)) for dx, dy in cross if dx != 0 and dy != 0]
    for peer in peers:
        pl.semaphore_signal(barrier, inc=1, device_id=peer, device_id_type=MESH)

    sv[...] = (vel[...] - MID).astype(BF16)
    pl.semaphore_wait(barrier, len(peers))

    sent = []
    first = []
    for side, step in ((0, 1), (1, -1)):
        target = slab_at(step)
        edge = pl.ds(4, 4) if step == 1 else pl.ds(0, 4)
        for f, (now, old) in enumerate(((cur, prev), (acur, anext))):
            first.append(send(now.at[0], rc.at[side, f], init_s.at[side, 2 * f], init_r.at[side, 2 * f], s, target))
            first.append(send(old.at[0, edge], rp.at[side, f], init_s.at[side, 2 * f + 1], init_r.at[side, 2 * f + 1], s, target))
        first.append(send(sv, rv.at[1 + side], init_s.at[side, 4], init_r.at[side, 4], s, target))
    far = []
    for side, step in ((0, 2), (1, -2)):
        far.append(send(sv, rv.at[3 * side], init_s.at[side, 5], init_r.at[side, 5], s, slab_at(step)))
    sent += first + far

    lane = lax.broadcasted_iota(jnp.int32, (64, 128), 1)
    diff = jnp.abs(lax.broadcasted_iota(jnp.int32, (128, 128), 0) - lax.broadcasted_iota(jnp.int32, (128, 128), 1))
    band = jnp.where(diff == 0, 3.0 * COEFFS[0], 0.0)
    for m in range(1, 5):
        band = jnp.where(diff == m, COEFFS[m], band)
    band_h, band_l = split(band, 2)
    bands[0:128, :] = band_h
    bands[128:256, :] = band_h
    bandl[...] = band_l

    for ref in (u0, u1, wa0, wa1, da, db):
        ref[:, 0:TOP, :] = jnp.zeros((ref.shape[0], TOP, 128), F32)
        ref[:, TOP + ROWS:, :] = jnp.zeros((ref.shape[0], 8, 128), F32)
    db[:, YS, :] = jnp.zeros((db.shape[0], ROWS, 128), F32)
    u0[8:16, YS, :] = cur[0].astype(F32)
    u1[8:16, YS, :] = acur[0].astype(F32)
    wa0[8:16, YS, :] = prev[0].astype(F32)
    wa1[8:16, YS, :] = anext[0].astype(F32)
    scaled = vel[...] * COURANT
    kap[16:24] = scaled * scaled

    cells = rec[...]
    rec_row = lax.shift_right_logical(cells, 7)
    rec_lane = cells & 127
    sub = lax.broadcasted_iota(jnp.int32, (8, 256), 0)
    digits = jnp.where(sub == 0, lax.shift_right_logical(rec_row, 6),
                       jnp.where(sub == 1, rec_row & 63, jnp.where(sub == 2, rec_lane, 0)))
    eye = jnp.where(
        lax.broadcasted_iota(jnp.int32, (256, 256), 0) == lax.broadcasted_iota(jnp.int32, (256, 256), 1),
        1.0, 0.0).astype(BF16)
    columns = lax.dot_general(eye, digits.astype(F32).astype(BF16), NT, preferred_element_type=F32)
    row_col = columns[:, 0:1] * 64.0 + columns[:, 1:2] - (b * 256).astype(F32)
    lane_col = columns[:, 2:3]
    lane_hot[...] = jnp.where(lane_col == lax.broadcasted_iota(jnp.int32, (256, 128), 1).astype(F32), 1.0, 0.0)
    pick[...] = jnp.where(
        row_col == lax.broadcasted_iota(jnp.int32, (256, 256), 1).astype(F32), 1.0, 0.0).astype(BF16)
    relative = rec_row - (b * 256 - 20 * ROWS)
    for q in range(6):
        hot[256 * q:256 * q + 256, :] = jnp.where(
            lax.broadcasted_iota(jnp.int32, (256, 256), 0) + 256 * q == relative, 1.0, 0.0).astype(BF16)
    cell = src[0]
    src_plane = lax.shift_right_logical(cell, 12)
    src_row = lax.shift_right_logical(cell, 7) & 31
    src_lane = cell & 127
    src_hot[...] = jnp.where(
        (lax.broadcasted_iota(jnp.int32, (ROWS, 128), 0) == src_row)
        & (lax.broadcasted_iota(jnp.int32, (ROWS, 128), 1) == src_lane), 1.0, 0.0)

    def z_pass(field, lo, n):
        for c in range(n // 8):
            x = field[lo + 8 * c:lo + 8 * c + 8, YS, :].reshape(256, 128)
            hi, low = split(x, 2)
            z = dot(jnp.concatenate([hi, low], axis=1), bands[...]) + dot(hi, bandl[...])
            zs[8 * c:8 * c + 8] = z.reshape(8, ROWS, 128)

    def advance(field, old, lo, n, kap_lo, extra):
        def one(i, carry):
            j = lo + i
            here = field[j, YS, :]
            acc = zs[i]
            for m in range(1, 5):
                around = (field[j + m, YS, :] + field[j - m, YS, :]) + (
                    field[j, TOP + m:TOP + m + ROWS, :] + field[j, TOP - m:TOP - m + ROWS, :])
                acc = acc + COEFFS[m] * around
            new = 2.0 * here - old[j, YS, :] + kap[kap_lo + i] * acc
            old[j, YS, :] = extra(i, j, new, acc)
            return carry
        lax.fori_loop(0, n, one, 0, unroll=2)

    def plain(i, j, new, acc):
        return new

    def forward_extra(n, keep_lo):
        weight = wav[0, n]
        first_plane = b * 8 - 8

        def extra(i, j, new, acc):
            zs[i] = acc
            amount = jnp.where(src_plane == first_plane + j, weight, 0.0)
            return new + src_hot[...] * amount
        return extra

    def sample(field, n):
        x = field[8:16, YS, :].reshape(256, 128)
        g = dot(pick[...], jnp.concatenate(split(x, 3), axis=1))
        hot3 = jnp.concatenate([lane_hot[...]] * 3, axis=1)
        values = lax.dot_general(jnp.ones((8, 384), BF16), (g * hot3).astype(BF16), NT, preferred_element_type=F32)
        tr[n:n + 1, :] = values[0:1, :]

    tr[...] = jnp.zeros((8, 256), F32)
    left, right = inside(-1), inside(1)
    for copy in first:
        copy.wait_recv()
    for f, (now, old) in enumerate(((u0, wa0), (u1, wa1))):
        now[0:8, YS, :] = rc[0, f].astype(F32) * left
        now[16:24, YS, :] = rc[1, f].astype(F32) * right
        old[4:8, YS, :] = rp[0, f].astype(F32) * left
        old[16:20, YS, :] = rp[1, f].astype(F32) * right

    def kappa_of(slot, valid):
        value = (rv[slot].astype(F32) + MID) * COURANT
        return value * value * valid

    kap[8:16] = kappa_of(1, left)
    kap[24:32] = kappa_of(2, right)

    for r in range(3):
        n = 2 * r
        z_pass(u0, 4, 16)
        advance(u0, wa0, 4, 16, 12, forward_extra(n, 4))
        lap[n] = zs[4:12]
        z_pass(wa0, 8, 8)
        advance(wa0, u0, 8, 8, 16, forward_extra(n + 1, 0))
        lap[n + 1] = zs[0:8]
        z_pass(u1, 4, 16)
        advance(u1, wa1, 4, 16, 12, plain)
        z_pass(wa1, 8, 8)
        advance(wa1, u1, 8, 8, 16, plain)
        if r < 2:
            sb[r, 0] = u0[8:16, YS, :].astype(BF16)
            sb[r, 1] = u1[8:16, YS, :].astype(BF16)
            copies = [
                send(sb.at[r], rb.at[r, side], round_s.at[r, side], round_r.at[r, side], s, slab_at(step))
                for side, step in ((0, 1), (1, -1))]
            sent += copies
        sample(wa0, n)
        sample(u0, n + 1)
        hom[STEPS - 1 - n] = wa1[8:16, YS, :]
        hom[STEPS - 2 - n] = u1[8:16, YS, :]
        if r < 2:
            for copy in copies:
                copy.wait_recv()
            for f, now in enumerate((u0, u1)):
                now[0:8, YS, :] = rb[r, 0, f].astype(F32) * left
                now[16:24, YS, :] = rb[r, 1, f].astype(F32) * right

    for k in range(1, slabs):
        send(tr, rt.at[k - 1], tr_s, tr_r, s, slab_at(k))
    image = hom[0] * lap[0]
    for n in range(1, STEPS):
        image = image + hom[n] * lap[n]
    img[...] = image
    for copy in far:
        copy.wait_recv()
    kap[0:8] = kappa_of(0, inside(-2))
    kap[32:40] = kappa_of(3, inside(2))
    pltpu.make_async_copy(rt, rt, tr_r).wait()
    total = tr[...]
    for k in range(slabs - 1):
        total = total + rt[k]
    traces = total[0:STEPS] - obs[0]
    mis[0] = traces
    mf[...] = jnp.zeros((8, 256), F32)
    mf[0:STEPS, :] = traces
    amounts = jnp.zeros((256, 8), F32)
    for part in split(mf[...], 3):
        amounts = amounts + lax.dot_general(eye, part, NT, preferred_element_type=F32)

    def inject(n, plane, planes):
        parts = split(amounts[:, n:n + 1] * lane_hot[...], 2)
        rhs = jnp.concatenate(parts, axis=1)
        for c in range(planes // 8):
            start = (plane + 8 * c) * ROWS
            both = dot(hot[start:start + 256, :], rhs)
            yield c, (both[:, 0:128] + both[:, 128:256]).reshape(8, ROWS, 128)

    for c, values in inject(5, 0, 48):
        da[8 * c:8 * c + 8, YS, :] = values
    img[...] += da[20:28, YS, :] * lap[5]

    def with_misfit(i, j, new, acc):
        return new + js[i]

    near, old = da, db
    for n in range(4, -1, -1):
        reach = 4 * n
        lo, planes = 20 - reach, 8 + 2 * reach
        z_pass(near, lo, planes)
        for c, values in inject(n, lo, planes):
            js[8 * c:8 * c + 8] = values
        advance(near, old, lo, planes, lo - 4, with_misfit)
        near, old = old, near
        img[...] += near[20:28, YS, :] * lap[n]

    imgt[...] = jnp.swapaxes(img[...], 0, 1)
    for k in range(1, shots):
        send(imgt.at[shot_at(k)], ri.at[k - 1], im_s, im_r, shot_at(k), b)
    mine = lax.broadcasted_iota(jnp.int32, (8, ROWS, 128), 1) == s
    own_velocity = jnp.sum(jnp.where(mine, vel[...], 0.0), axis=1)
    pltpu.make_async_copy(ri, ri, im_r).wait()
    summed = imgt[s]
    for k in range(shots - 1):
        summed = summed + ri[k]
    update = RATE * (summed / shots)
    moved = own_velocity - update
    fs[0:8, :] = (moved - CENTER).astype(BF16)
    fs[8:16, :] = update.astype(BF16)

    for slot, (dx, dy) in enumerate(cross):
        send(fs, rf.at[slot], ft_s, ft_r, shot_at(-dy), slab_at(-dx))
    pltpu.make_async_copy(rf, rf, ft_r).wait()

    def row_inside(k):
        return jnp.where((s + k >= 0) & (s + k < shots), 1.0, 0.0).astype(F32)

    for slot, (dx, dy) in enumerate(cross):
        valid = inside(dx) * row_inside(dy)
        feat[(dy + 3) * 3 + dx + 1] = (rf[slot].astype(F32) * valid).astype(BF16)
    feat[10] = fs[...]

    def first_conv(y, carry):
        g1[...] = dot(w1[...], feat[pl.ds(3 * y, 9)].reshape(144, 128))
        row_ok = jnp.where((s + y - 2 >= 0) & (s + y - 2 < shots), 1.0, 0.0)

        def one(x, carry):
            plane = b * 8 + x - 2
            ok = jnp.where((plane >= 0) & (plane < slabs * 8), row_ok, 0.0)
            g = g1[pl.ds(pl.multiple_of(x * 192, 192), 192), :]
            value = jnp.maximum(z_combine(g, lane) + b1[...], 0.0) * ok
            h1[y, x] = value.astype(BF16)
            return carry
        lax.fori_loop(0, 12, one, 0, unroll=2)
        return carry

    lax.fori_loop(0, 5, first_conv, 0)

    def second_conv(i, carry):
        y = i // 5
        x0 = 2 * (i - 5 * y)
        halves = []
        for x in (x0, x0 + 1):
            halves.append(jnp.concatenate([h1[y + j, pl.ds(x, 3)].reshape(192, 128) for j in range(3)], axis=0))
        g = dot(wm[...], jnp.concatenate(halves, axis=1))
        row_ok = jnp.where((s + y - 1 >= 0) & (s + y - 1 < shots), 1.0, 0.0)
        for half in range(2):
            x = x0 + half
            plane = b * 8 + x - 1
            ok = jnp.where((plane >= 0) & (plane < slabs * 8), row_ok, 0.0)
            value = jnp.maximum(z_combine(g[:, 128 * half:128 * half + 128], lane) + b2[...], 0.0) * ok
            h2[y, x] = value.astype(BF16)
        return carry

    lax.fori_loop(0, 15, second_conv, 0)

    lane1 = lax.broadcasted_iota(jnp.int32, (1, 128), 1)
    for x in range(8):
        rhs = jnp.concatenate([h2[j, x:x + 3].reshape(192, 128) for j in range(3)], axis=0)
        g = dot(w3[...], rhs)
        low = jnp.where(lane1 == 0, 0.0, pltpu.roll(g[0:8], 1, 1)[0:1])
        high = jnp.where(lane1 == 127, 0.0, pltpu.roll(g[0:8], 127, 1)[2:3])
        row[x:x + 1, :] = moved[x:x + 1] + (g[1:2] + low + high + b3[0])

    for k in range(1, shots):
        send(row, ro.at[k - 1], ou_s, ou_r, shot_at(k), b)
    out[s] = row[...]
    pltpu.make_async_copy(ro, ro, ou_r).wait()
    for k in range(1, shots):
        out[shot_at(-k)] = ro[k - 1]

    for copy in sent:
        copy.wait_send()
    pltpu.make_async_copy(rt, rt, tr_s).wait()
    pltpu.make_async_copy(ri, ri, im_s).wait()
    pltpu.make_async_copy(rf, rf, ft_s).wait()
    pltpu.make_async_copy(ro, ro, ou_s).wait()


def band_weights(weight_in):
    w = weight_in.reshape(3, 3, 3, 2, 64)
    x = jnp.arange(12)[None, :]
    plane = jnp.arange(24)[None, None, :] - 8
    tap = jnp.arange(3)[:, None]
    select = (plane - (x - 2)[:, :, None] + 1 == tap[:, :, None]).astype(BF16)
    select = select.reshape(3, 12, 3, 8)
    wide = jnp.einsum("ijkco,ixdp->xkojdcp", w, select)
    return wide.reshape(12 * 192, 144)


def shards(slabs, shots, previous_field, current_field, adjoint_next, adjoint_current, velocity, wavelet, source_cell,
           receiver_cell, observed, weight_in, bias_in, weight_mid, bias_mid, weight_out, bias_out):
    w1 = band_weights(weight_in)
    wm = jnp.transpose(weight_mid.reshape(3, 3, 3, 64, 64), (2, 4, 1, 0, 3)).reshape(192, 576)
    w3 = jnp.transpose(weight_out.reshape(3, 3, 3, 64), (2, 1, 0, 3)).reshape(3, 576)
    w3 = jnp.pad(w3, ((0, 13), (0, 0)))
    vmem = pl.BlockSpec(memory_space=pltpu.VMEM)
    smem = pl.BlockSpec(memory_space=pltpu.SMEM)
    f32 = lambda *shape: pltpu.VMEM(shape, F32)
    bf = lambda *shape: pltpu.VMEM(shape, BF16)
    dma = pltpu.SemaphoreType.DMA
    scratch = [
        f32(24, 48, 128), f32(24, 48, 128), f32(24, 48, 128), f32(24, 48, 128),
        f32(48, 48, 128), f32(48, 48, 128), f32(40, 32, 128), f32(40, 32, 128), f32(40, 32, 128),
        f32(6, 8, 32, 128), f32(6, 8, 32, 128), f32(8, 32, 128), f32(32, 8, 128),
        bf(8, 32, 128), bf(4, 8, 32, 128), bf(2, 2, 8, 32, 128), bf(2, 2, 4, 32, 128),
        bf(2, 2, 8, 32, 128), bf(2, 2, 2, 8, 32, 128),
        f32(8, 256), f32(slabs - 1, 8, 256), f32(8, 256),
        bf(1536, 256), bf(256, 256), f32(256, 128), f32(32, 128), bf(256, 128), bf(128, 128),
        f32(shots - 1, 8, 128), bf(16, 128), bf(20, 16, 128), bf(21, 16, 128), f32(2304, 128),
        bf(5, 12, 64, 128), bf(3, 10, 64, 128), f32(8, 128), f32(shots - 1, 8, 128),
        dma((2, 6)), dma((2, 6)), dma((2, 2)), dma((2, 2)),
    ] + [dma] * 8
    rows, misfit = pl.pallas_call(
        functools.partial(kernel, slabs, shots),
        out_shape=(jax.ShapeDtypeStruct((shots, 8, 128), F32), jax.ShapeDtypeStruct((1, 6, 256), F32)),
        in_specs=[vmem, vmem, vmem, vmem, vmem, smem, smem, vmem, vmem, vmem, vmem, vmem, vmem, vmem, smem],
        out_specs=(vmem, vmem),
        scratch_shapes=scratch,
        compiler_params=pltpu.CompilerParams(
            collective_id=0, has_side_effects=True, vmem_limit_bytes=60 * 1024 * 1024),
    )(previous_field, current_field, adjoint_next, adjoint_current, velocity, wavelet, source_cell, receiver_cell,
      observed, w1, bias_in[:, None], wm, bias_mid[:, None], w3, bias_out)
    return jnp.swapaxes(rows, 0, 1), misfit


def solution(mesh):
    placed = (
        P("shot", "slab", None, None), P("shot", "slab", None, None), P("shot", "slab", None, None),
        P("shot", "slab", None, None), P("slab", None, None), P("shot", None), P("shot"), P("shot", None),
        P("shot", None, None), P(), P(), P(), P(), P(), P(),
    )
    return jax.shard_map(
        functools.partial(shards, mesh.shape["slab"], mesh.shape["shot"]),
        mesh=mesh,
        in_specs=placed,
        out_specs=(P("slab", None, None), P("shot", None, None)),
        check_vma=False,
    )
```

```python
import functools

import jax
import jax.numpy as jnp
from jax import lax
from jax.experimental import pallas as pl
from jax.experimental.pallas import tpu as pltpu
from jax.sharding import PartitionSpec as P

COEFFS = (-205.0 / 72.0, 8.0 / 5.0, -1.0 / 5.0, 8.0 / 315.0, -1.0 / 560.0)
COURANT = 0.1
RATE = 0.2
CENTER = 3.0
MID = 2.75
MESH = pl.DeviceIdType.MESH
F32 = jnp.float32
BF16 = jnp.bfloat16
NT = (((1,), (1,)), ((), ()))
STEPS = 6
TOP, ROWS = 8, 32
YS = slice(TOP, TOP + ROWS)


def dot(a, b):
    return jnp.dot(a, b, preferred_element_type=F32)


def split(x, pieces):
    parts = []
    for _ in range(pieces):
        part = x.astype(BF16)
        parts.append(part)
        x = x - part.astype(F32)
    return parts


def z_combine(g, lane):
    low = jnp.where(lane == 0, 0.0, pltpu.roll(g[0:64], 1, 1))
    high = jnp.where(lane == 127, 0.0, pltpu.roll(g[128:192], 127, 1))
    return g[64:128] + low + high


def kernel(
    slabs, shots,
    wav, src, b3, *refs,
):
    hbm, (out, mis), loaded, rest = refs[:12], refs[12:14], refs[14:26], refs[26:]
    prev, cur, anext, acur, vel, rec, obs, wi, bi, wd, bd, wo = loaded
    (
        u0, u1, wa0, wa1, da, db, zs, js, kap, lap, hom, img, imgt, sv, vp, rv, rn, rc, rp, sb, rb, tr, rt, mf, hot, pick, lane_hot, src_hot, bands, bandl, ri, fs, rf, feat, wf, w1, wm, w3, widen, im, h1, h2, row, ro, init_s, init_r, vp_s, vp_r, rv_s, rv_r, round_s, round_r, tr_s, tr_r, im_s, im_r, ft_s, ft_r, ou_s, ou_r, load_s,
    ) = rest
    s = lax.axis_index("shot")
    b = lax.axis_index("slab")

    def shot_at(k):
        return lax.rem(s + k + shots, shots)

    def slab_at(k):
        return lax.rem(b + k + slabs, slabs)

    def inside(k):
        return jnp.where((b + k >= 0) & (b + k < slabs), 1.0, 0.0).astype(F32)

    def send(source, target, ss, rs, shot, slab):
        copy = pltpu.make_async_remote_copy(
            src_ref=source, dst_ref=target, send_sem=ss, recv_sem=rs,
            device_id=(shot, slab), device_id_type=MESH)
        copy.start()
        return copy

    barrier = pltpu.get_barrier_semaphore()
    peers = [(s, slab_at(k)) for k in range(1, slabs)]
    peers += [(shot_at(k), b) for k in range(1, shots)]
    cross = [(dx, dy) for dy in range(-3, 4) for dx in (-1, 0, 1) if (dx, dy) != (0, 0)]
    peers += [(shot_at(dy), slab_at(dx)) for dx, dy in cross if dx != 0 and dy != 0]
    for peer in peers:
        pl.semaphore_signal(barrier, inc=1, device_id=peer, device_id_type=MESH)

    loads = [pltpu.make_async_copy(hbm[at], loaded[at], load_s.at[at]) for at in range(12)]
    for at in (4, 1, 0, 3, 2, 5, 6, 7, 8, 9, 10, 11):
        loads[at].start()
    loads[4].wait()
    sv[...] = (vel[...] - MID).astype(BF16)
    for at in (0, 1, 2, 3):
        loads[at].wait()
    pl.semaphore_wait(barrier, len(peers))

    zi = lax.rem(lax.div(s, 2), 8)
    sent = []
    first = ([], [])
    for f, (now, old) in enumerate(((cur, prev), (acur, anext))):
        for side, step in ((0, 1), (1, -1)):
            target = slab_at(step)
            edge = pl.ds(4, 4) if step == 1 else pl.ds(0, 4)
            at = init_s.at[side, 2 * f], init_r.at[side, 2 * f]
            first[f].append(send(now.at[0], rc.at[side, f], *at, s, target))
            at = init_s.at[side, 2 * f + 1], init_r.at[side, 2 * f + 1]
            first[f].append(send(old.at[0, edge], rp.at[side, f], *at, s, target))
            if f == 0:
                first[f].append(send(sv.at[edge], rn.at[side], init_s.at[side, 4], init_r.at[side, 4], s, target))
    for slot, step in enumerate((2, 1, -1, -2)):
        send(sv.at[zi], vp.at[slot], vp_s, vp_r, s, slab_at(step))
    sent += first[0] + first[1]

    for at in range(5, 12):
        loads[at].wait()
    lane = lax.broadcasted_iota(jnp.int32, (64, 128), 1)
    diff = jnp.abs(lax.broadcasted_iota(jnp.int32, (128, 128), 0) - lax.broadcasted_iota(jnp.int32, (128, 128), 1))
    band = jnp.where(diff == 0, 3.0 * COEFFS[0], 0.0)
    for m in range(1, 5):
        band = jnp.where(diff == m, COEFFS[m], band)
    band_h, band_l = split(band, 2)
    bands[0:128, :] = band_h
    bands[128:256, :] = band_h
    bandl[...] = band_l

    for ref in (u0, u1, wa0, wa1, da, db):
        ref[:, 0:TOP, :] = jnp.zeros((ref.shape[0], TOP, 128), F32)
        ref[:, TOP + ROWS:, :] = jnp.zeros((ref.shape[0], 8, 128), F32)
    db[:, YS, :] = jnp.zeros((db.shape[0], ROWS, 128), F32)
    u0[8:16, YS, :] = cur[0].astype(F32)
    u1[8:16, YS, :] = acur[0].astype(F32)
    wa0[8:16, YS, :] = prev[0].astype(F32)
    wa1[8:16, YS, :] = anext[0].astype(F32)
    scaled = vel[...] * COURANT
    kap[16:24] = scaled * scaled

    cells = rec[...]
    rec_row = lax.shift_right_logical(cells, 7)
    rec_lane = cells & 127
    sub = lax.broadcasted_iota(jnp.int32, (8, 256), 0)
    digits = jnp.where(sub == 0, lax.shift_right_logical(rec_row, 6),
                       jnp.where(sub == 1, rec_row & 63, jnp.where(sub == 2, rec_lane, 0)))
    eye = jnp.where(
        lax.broadcasted_iota(jnp.int32, (256, 256), 0) == lax.broadcasted_iota(jnp.int32, (256, 256), 1),
        1.0, 0.0).astype(BF16)
    columns = lax.dot_general(eye, digits.astype(F32).astype(BF16), NT, preferred_element_type=F32)
    row_col = columns[:, 0:1] * 64.0 + columns[:, 1:2] - (b * 256).astype(F32)
    lane_col = columns[:, 2:3]
    lane_hot[...] = jnp.where(lane_col == lax.broadcasted_iota(jnp.int32, (256, 128), 1).astype(F32), 1.0, 0.0)
    pick[...] = jnp.where(
        row_col == lax.broadcasted_iota(jnp.int32, (256, 256), 1).astype(F32), 1.0, 0.0).astype(BF16)
    relative = rec_row - (b * 256 - 20 * ROWS)
    for q in range(6):
        hot[256 * q:256 * q + 256, :] = jnp.where(
            lax.broadcasted_iota(jnp.int32, (256, 256), 0) + 256 * q == relative, 1.0, 0.0).astype(BF16)
    cell = src[0]
    src_plane = lax.shift_right_logical(cell, 12)
    src_row = lax.shift_right_logical(cell, 7) & 31
    src_lane = cell & 127
    src_hot[...] = jnp.where(
        (lax.broadcasted_iota(jnp.int32, (ROWS, 128), 0) == src_row)
        & (lax.broadcasted_iota(jnp.int32, (ROWS, 128), 1) == src_lane), 1.0, 0.0)

    def iota(rows, columns, axis):
        return lax.broadcasted_iota(jnp.int32, (rows, columns), axis)

    def one_hot(condition):
        return jnp.where(condition, 1.0, 0.0).astype(BF16)

    eye64 = one_hot(iota(64, 64, 0) == iota(64, 64, 1))
    wf[...] = jnp.zeros((96, 64), F32)
    for t in range(27):
        wf[2 * t:2 * t + 2, :] = wi[t].astype(F32)
    wf[64:91, :] = wo[...].astype(F32)
    taps_in = wf[0:64, :].astype(BF16)
    taps_out = wf[64:96, :].astype(BF16)
    q = iota(96, 64, 0)
    i, j, c = (q >> 3) & 3, (q >> 1) & 3, q & 1
    wanted = one_hot((iota(96, 64, 1) == (9 * i + 3 * j + (q >> 5)) * 2 + c) & (i < 3) & (j < 3))
    chosen = dot(wanted, taps_in).astype(BF16)
    w1[...] = lax.dot_general(eye64, chosen, NT, preferred_element_type=F32).astype(BF16)
    for k in range(3):
        for u in range(0, 9, 2):
            pair = [wd[9 * (v % 3) + 3 * (v // 3) + k] for v in range(u, min(u + 2, 9))]
            both = lax.dot_general(eye64, jnp.concatenate(pair, axis=0), NT, preferred_element_type=F32)
            wm[64 * k:64 * k + 64, 64 * u:64 * (u + len(pair))] = both.astype(BF16)
    for u in range(0, 9, 2):
        both = jnp.zeros((16, 128), F32)
        for v in range(u, min(u + 2, 9)):
            wanted = one_hot((iota(16, 32, 1) == 9 * (v % 3) + 3 * (v // 3) + iota(16, 32, 0)) & (iota(16, 32, 0) < 3))
            place = one_hot(iota(64, 128, 1) == iota(64, 128, 0) + 64 * (v - u))
            both = both + dot(dot(wanted, taps_out).astype(BF16), place)
        w3[:, 64 * u:min(64 * u + 128, 576)] = both[:, 0:min(128, 576 - 64 * u)].astype(BF16)
    sub64 = iota(8, 64, 0)
    biases = jnp.zeros((8, 64), F32)
    for at, part in enumerate(split(bi[...], 3) + split(bd[...], 3)):
        biases = jnp.where(sub64 == at, part.astype(F32), biases)
    bias_col = lax.dot_general(eye64, biases.astype(BF16), NT, preferred_element_type=F32)
    b1 = bias_col[:, 0:1] + bias_col[:, 1:2] + bias_col[:, 2:3]
    b2 = bias_col[:, 3:4] + bias_col[:, 4:5] + bias_col[:, 5:6]
    r, col = iota(384, 144, 0), iota(384, 144, 1)
    group = jnp.where(col >= 48, 1, 0) + jnp.where(col >= 96, 1, 0)
    rest = col - 48 * group
    part_of = rest >> 4
    widen[...] = one_hot(
        (((r >> 1) & 3) == group) & ((r & 1) == ((rest >> 3) & 1)) & (((r >> 3) & 3) < 3)
        & (8 * part_of + (rest & 7) == (r >> 5) + ((r >> 3) & 3) + 5))

    def z_pass(field, lo, n):
        for c in range(n // 8):
            x = field[lo + 8 * c:lo + 8 * c + 8, YS, :].reshape(256, 128)
            hi, low = split(x, 2)
            z = dot(jnp.concatenate([hi, low], axis=1), bands[...]) + dot(hi, bandl[...])
            zs[8 * c:8 * c + 8] = z.reshape(8, ROWS, 128)

    def advance(field, old, lo, n, kap_lo, extra):
        def one(i, carry):
            j = lo + i
            here = field[j, YS, :]
            acc = zs[i]
            for m in range(1, 5):
                around = (field[j + m, YS, :] + field[j - m, YS, :]) + (
                    field[j, TOP + m:TOP + m + ROWS, :] + field[j, TOP - m:TOP - m + ROWS, :])
                acc = acc + COEFFS[m] * around
            new = 2.0 * here - old[j, YS, :] + kap[kap_lo + i] * acc
            old[j, YS, :] = extra(i, j, new, acc)
            return carry
        lax.fori_loop(0, n, one, 0, unroll=2)

    def plain(i, j, new, acc):
        return new

    def forward_extra(n):
        weight = wav[0, n]
        first_plane = b * 8 - 8

        def extra(i, j, new, acc):
            zs[i] = acc
            amount = jnp.where(src_plane == first_plane + j, weight, 0.0)
            return new + src_hot[...] * amount
        return extra

    def sample(field, n):
        x = field[8:16, YS, :].reshape(256, 128)
        g = dot(pick[...], jnp.concatenate(split(x, 3), axis=1))
        hot3 = jnp.concatenate([lane_hot[...]] * 3, axis=1)
        values = lax.dot_general(jnp.ones((8, 384), BF16), (g * hot3).astype(BF16), NT, preferred_element_type=F32)
        tr[n:n + 1, :] = values[0:1, :]

    tr[...] = jnp.zeros((8, 256), F32)
    left, right = inside(-1), inside(1)

    def kappa_of(values, valid):
        value = (values.astype(F32) + MID) * COURANT
        return value * value * valid

    def fill(now, from_left, from_right):
        now[0:8, YS, :] = from_left.astype(F32) * left
        now[16:24, YS, :] = from_right.astype(F32) * right

    fields = ((u0, wa0), (u1, wa1))
    copies = [None, None]

    def round_of(r, f):
        now, old = fields[f]
        if r == 0:
            for copy in first[f]:
                copy.wait_recv()
            fill(now, rc[0, f], rc[1, f])
            old[4:8, YS, :] = rp[0, f].astype(F32) * left
            old[16:20, YS, :] = rp[1, f].astype(F32) * right
            if f == 0:
                kap[12:16] = kappa_of(rn[0], left)
                kap[24:28] = kappa_of(rn[1], right)
        else:
            for copy in copies[f]:
                copy.wait_recv()
            fill(now, rb[r - 1, f, 0], rb[r - 1, f, 1])
        n = 2 * r
        z_pass(now, 4, 16)
        advance(now, old, 4, 16, 12, plain if f else forward_extra(n))
        if f == 0:
            lap[n] = zs[4:12]
        z_pass(old, 8, 8)
        advance(old, now, 8, 8, 16, plain if f else forward_extra(n + 1))
        if f == 0:
            lap[n + 1] = zs[0:8]
        if r < 2:
            sb[r, f] = now[8:16, YS, :].astype(BF16)
            copies[f] = [
                send(sb.at[r, f], rb.at[r, f, side], round_s.at[2 * r + f, side], round_r.at[2 * r + f, side],
                     s, slab_at(step))
                for side, step in ((0, 1), (1, -1))]
            sent.extend(copies[f])
        if f == 0:
            sample(old, n)
            sample(now, n + 1)
        else:
            hom[STEPS - 1 - n] = old[8:16, YS, :]
            hom[STEPS - 2 - n] = now[8:16, YS, :]

    round_of(0, 0)
    pltpu.make_async_copy(vp, vp, vp_r).wait()
    for k in range(1, 8):
        send(vp, rv.at[k - 1], rv_s, rv_r, s + 2 * (lax.rem(zi + k, 8) - zi), b)
    round_of(0, 1)
    round_of(1, 0)
    round_of(1, 1)
    round_of(2, 0)

    for k in range(1, slabs):
        send(tr, rt.at[k - 1], tr_s, tr_r, s, slab_at(k))
    round_of(2, 1)
    image = hom[0] * lap[0]
    for n in range(1, STEPS):
        image = image + hom[n] * lap[n]
    img[...] = image
    pltpu.make_async_copy(rv, rv, rv_r).wait()
    near_far = ((0, inside(-2)), (8, left), (24, right), (32, inside(2)))
    for k in range(8):
        plane = lax.rem(zi - k + 8, 8)
        for slot, (base, valid) in enumerate(near_far):
            kap[base + plane] = kappa_of(rv[k - 1, slot] if k else vp[slot], valid)
    pltpu.make_async_copy(rt, rt, tr_r).wait()
    total = tr[...]
    for k in range(slabs - 1):
        total = total + rt[k]
    mf[...] = jnp.zeros((8, 256), F32)
    for n in range(STEPS):
        trace = total[n:n + 1] - obs[n]
        mis[n] = trace
        mf[n:n + 1, :] = trace
    amounts = jnp.zeros((256, 8), F32)
    for part in split(mf[...], 3):
        amounts = amounts + lax.dot_general(eye, part, NT, preferred_element_type=F32)

    def inject(n, plane, planes):
        parts = split(amounts[:, n:n + 1] * lane_hot[...], 2)
        rhs = jnp.concatenate(parts, axis=1)
        for c in range(planes // 8):
            start = (plane + 8 * c) * ROWS
            both = dot(hot[start:start + 256, :], rhs)
            yield c, (both[:, 0:128] + both[:, 128:256]).reshape(8, ROWS, 128)

    for c, values in inject(5, 0, 48):
        da[8 * c:8 * c + 8, YS, :] = values
    img[...] += da[20:28, YS, :] * lap[5]

    def with_misfit(i, j, new, acc):
        return new + js[i]

    near, old = da, db
    for n in range(4, -1, -1):
        reach = 4 * n
        lo, planes = 20 - reach, 8 + 2 * reach
        z_pass(near, lo, planes)
        for c, values in inject(n, lo, planes):
            js[8 * c:8 * c + 8] = values
        advance(near, old, lo, planes, lo - 4, with_misfit)
        near, old = old, near
        img[...] += near[20:28, YS, :] * lap[n]

    imgt[...] = jnp.swapaxes(img[...], 0, 1)
    for k in range(1, shots):
        send(imgt.at[shot_at(k)], ri.at[k - 1], im_s, im_r, shot_at(k), b)
    mine = lax.broadcasted_iota(jnp.int32, (8, ROWS, 128), 1) == s
    own_velocity = jnp.sum(jnp.where(mine, vel[...], 0.0), axis=1)
    pltpu.make_async_copy(ri, ri, im_r).wait()
    summed = imgt[s]
    for k in range(shots - 1):
        summed = summed + ri[k]
    update = RATE * (summed / shots)
    moved = own_velocity - update
    fs[0:8, :] = (moved - CENTER).astype(BF16)
    fs[8:16, :] = update.astype(BF16)

    for slot, (dx, dy) in enumerate(cross):
        send(fs, rf.at[slot], ft_s, ft_r, shot_at(-dy), slab_at(-dx))
    pltpu.make_async_copy(rf, rf, ft_r).wait()

    def row_inside(k):
        return jnp.where((s + k >= 0) & (s + k < shots), 1.0, 0.0).astype(F32)

    lane16 = iota(16, 128, 1)

    def place_features(at, values):
        feat[at, :, 0:128] = jnp.where(lane16 == 0, 0.0, pltpu.roll(values, 1, 1)).astype(BF16)
        feat[at, :, 128:256] = values.astype(BF16)
        feat[at, :, 256:384] = jnp.where(lane16 == 127, 0.0, pltpu.roll(values, 127, 1)).astype(BF16)

    for slot, (dx, dy) in enumerate(cross):
        valid = inside(dx) * row_inside(dy)
        place_features((dy + 3) * 3 + dx + 1, rf[slot].astype(F32) * valid)
    place_features(10, fs[...].astype(F32))

    def first_conv(y, carry):
        spread = dot(widen[...], feat[pl.ds(3 * y, 9)].reshape(144, 384)).astype(BF16)
        for k in range(3):
            im[:, k] = spread[:, 128 * k:128 * k + 128].reshape(12, 32, 128)
        row_ok = jnp.where((s + y - 2 >= 0) & (s + y - 2 < shots), 1.0, 0.0)
        for x0 in range(0, 12, 2):
            g = dot(w1[...], jnp.concatenate([im[x0].reshape(96, 128), im[x0 + 1].reshape(96, 128)], axis=1))
            for half in range(2):
                plane = b * 8 + x0 + half - 2
                ok = jnp.where((plane >= 0) & (plane < slabs * 8), row_ok, 0.0)
                value = jnp.maximum(g[:, 128 * half:128 * half + 128] + b1, 0.0) * ok
                h1[y, x0 + half] = value.astype(BF16)
        return carry

    lax.fori_loop(0, 5, first_conv, 0)

    def second_conv(y, carry):
        row_ok = jnp.where((s + y - 1 >= 0) & (s + y - 1 < shots), 1.0, 0.0)
        for x0 in range(0, 10, 2):
            halves = []
            for x in (x0, x0 + 1):
                halves.append(jnp.concatenate([h1[y + j, x:x + 3].reshape(192, 128) for j in range(3)], axis=0))
            g = dot(wm[...], jnp.concatenate(halves, axis=1))
            for half in range(2):
                x = x0 + half
                plane = b * 8 + x - 1
                ok = jnp.where((plane >= 0) & (plane < slabs * 8), row_ok, 0.0)
                value = jnp.maximum(z_combine(g[:, 128 * half:128 * half + 128], lane) + b2, 0.0) * ok
                h2[y, x] = value.astype(BF16)
        return carry

    lax.fori_loop(0, 3, second_conv, 0)

    lane1 = lax.broadcasted_iota(jnp.int32, (1, 128), 1)
    for x in range(8):
        rhs = jnp.concatenate([h2[j, x:x + 3].reshape(192, 128) for j in range(3)], axis=0)
        g = dot(w3[...], rhs)
        low = jnp.where(lane1 == 0, 0.0, pltpu.roll(g[0:8], 1, 1)[0:1])
        high = jnp.where(lane1 == 127, 0.0, pltpu.roll(g[0:8], 127, 1)[2:3])
        row[x:x + 1, :] = moved[x:x + 1] + (g[1:2] + low + high + b3[0])

    for k in range(1, shots):
        send(row, ro.at[k - 1], ou_s, ou_r, shot_at(k), b)
    out[s] = row[...]
    pltpu.make_async_copy(ro, ro, ou_r).wait()
    for k in range(1, shots):
        out[shot_at(-k)] = ro[k - 1]

    for copy in sent:
        copy.wait_send()
    pltpu.make_async_copy(vp, vp, vp_s).wait()
    pltpu.make_async_copy(rv, rv, rv_s).wait()
    pltpu.make_async_copy(rt, rt, tr_s).wait()
    pltpu.make_async_copy(ri, ri, im_s).wait()
    pltpu.make_async_copy(rf, rf, ft_s).wait()
    pltpu.make_async_copy(ro, ro, ou_s).wait()


def shards(slabs, shots, previous_field, current_field, adjoint_next, adjoint_current, velocity, wavelet, source_cell,
           receiver_cell, observed, weight_in, bias_in, weight_mid, bias_mid, weight_out, bias_out):
    vmem = pl.BlockSpec(memory_space=pltpu.VMEM)
    smem = pl.BlockSpec(memory_space=pltpu.SMEM)
    f32 = lambda *shape: pltpu.VMEM(shape, F32)
    bf = lambda *shape: pltpu.VMEM(shape, BF16)
    dma = pltpu.SemaphoreType.DMA
    arrays = (previous_field, current_field, adjoint_next, adjoint_current, velocity, receiver_cell,
              jnp.swapaxes(observed, 0, 1), weight_in, bias_in[None], weight_mid, bias_mid[None], weight_out.reshape(27, 64))
    scratch = [pltpu.VMEM(a.shape, a.dtype) for a in arrays] + [
        f32(24, 48, 128), f32(24, 48, 128), f32(24, 48, 128), f32(24, 48, 128),
        f32(48, 48, 128), f32(48, 48, 128), f32(40, 32, 128), f32(40, 32, 128), f32(40, 32, 128),
        f32(6, 8, 32, 128), f32(6, 8, 32, 128), f32(8, 32, 128), f32(32, 8, 128),
        bf(8, 32, 128), bf(4, 32, 128), bf(7, 4, 32, 128), bf(2, 4, 32, 128), bf(2, 2, 8, 32, 128), bf(2, 2, 4, 32, 128),
        bf(2, 2, 8, 32, 128), bf(2, 2, 2, 8, 32, 128),
        f32(8, 256), f32(slabs - 1, 8, 256), f32(8, 256),
        bf(1536, 256), bf(256, 256), f32(256, 128), f32(32, 128), bf(256, 128), bf(128, 128),
        f32(shots - 1, 8, 128), bf(16, 128), bf(20, 16, 128), bf(21, 16, 384),
        f32(96, 64), bf(64, 96), bf(192, 576), bf(16, 576), bf(384, 144), bf(12, 3, 32, 128),
        bf(5, 12, 64, 128), bf(3, 10, 64, 128), f32(8, 128), f32(shots - 1, 8, 128),
        dma((2, 5)), dma((2, 5)), dma, dma, dma, dma, dma((4, 2)), dma((4, 2)),
    ] + [dma] * 8 + [dma((12,))]
    rows, misfit = pl.pallas_call(
        functools.partial(kernel, slabs, shots),
        out_shape=(jax.ShapeDtypeStruct((shots, 8, 128), F32), jax.ShapeDtypeStruct((STEPS, 1, 256), F32)),
        in_specs=[smem, smem, smem] + [pl.BlockSpec(memory_space=pl.ANY)] * 12,
        out_specs=(vmem, vmem),
        scratch_shapes=scratch,
        compiler_params=pltpu.CompilerParams(
            collective_id=0, has_side_effects=True, vmem_limit_bytes=60 * 1024 * 1024),
    )(wavelet, source_cell, bias_out, *arrays)
    return jnp.swapaxes(rows, 0, 1), jnp.swapaxes(misfit, 0, 1)


def solution(mesh):
    placed = (
        P("shot", "slab", None, None), P("shot", "slab", None, None), P("shot", "slab", None, None),
        P("shot", "slab", None, None), P("slab", None, None), P("shot", None), P("shot"), P("shot", None),
        P("shot", None, None), P(), P(), P(), P(), P(), P(),
    )
    return jax.shard_map(
        functools.partial(shards, mesh.shape["slab"], mesh.shape["shot"]),
        mesh=mesh,
        in_specs=placed,
        out_specs=(P("slab", None, None), P("shot", None, None)),
        check_vma=False,
    )
```

```python
import functools

import jax
import jax.numpy as jnp
from jax import lax
from jax.experimental import pallas as pl
from jax.experimental.pallas import tpu as pltpu
from jax.sharding import PartitionSpec as P

COEFFS = (-205.0 / 72.0, 8.0 / 5.0, -1.0 / 5.0, 8.0 / 315.0, -1.0 / 560.0)
COURANT = 0.1
RATE = 0.2
CENTER = 3.0
MID = 2.75
MESH = pl.DeviceIdType.MESH
F32 = jnp.float32
BF16 = jnp.bfloat16
NT = (((1,), (1,)), ((), ()))
STEPS = 6
TOP, ROWS = 8, 32
YS = slice(TOP, TOP + ROWS)


def dot(a, b):
    return jnp.dot(a, b, preferred_element_type=F32)


def split(x, pieces):
    parts = []
    for _ in range(pieces):
        part = x.astype(BF16)
        parts.append(part)
        x = x - part.astype(F32)
    return parts


def z_combine(g, lane):
    low = jnp.where(lane == 0, 0.0, pltpu.roll(g[0:64], 1, 1))
    high = jnp.where(lane == 127, 0.0, pltpu.roll(g[128:192], 127, 1))
    return g[64:128] + low + high


def kernel(
    slabs, shots,
    wav, src, b3, *refs,
):
    hbm, (out, mis), loaded, rest = refs[:12], refs[12:14], refs[14:26], refs[26:]
    prev, cur, anext, acur, vel, rec, obs, wi, bi, wd, bd, wo = loaded
    (
        u0, u1, wa0, wa1, da, db, zs, js, kap, lap, hom, img, imgt, ip, chip_sum, sv, vp, rv, rn, rc, rp, sb, rb, tr, rt, mf, hot, pick, lane_hot, src_hot, bands, bandl, ri, fs, rf, feat, wf, w1, wm, w3, widen, im, h1, h2, row, ro, init_s, init_r, vp_s, vp_r, rv_s, rv_r, round_s, round_r, tr_s, tr_r, im_s, im_r, ft_s, ft_r, ou_s, ou_r, load_s, ip_s, ip_r,
        token_slab2, token_slab4, token_z, token_core, token_half, token_beside,
    ) = rest
    s = lax.axis_index("shot")
    b = lax.axis_index("slab")

    def shot_at(k):
        return lax.rem(s + k + shots, shots)

    def slab_at(k):
        return lax.rem(b + k + slabs, slabs)

    def inside(k):
        return jnp.where((b + k >= 0) & (b + k < slabs), 1.0, 0.0).astype(F32)

    def send(source, target, ss, rs, shot, slab):
        copy = pltpu.make_async_remote_copy(
            src_ref=source, dst_ref=target, send_sem=ss, recv_sem=rs,
            device_id=(shot, slab), device_id_type=MESH)
        copy.start()
        return copy

    cross = [(dx, dr) for dr in range(-2, 3) for dx in (-1, 0, 1) if (dx, dr) != (0, 0)]

    barrier = pltpu.get_barrier_semaphore()
    zi = lax.rem(lax.div(s, 2), 8)
    pair = lax.rem(s, 16)
    half = s - pair

    def z_at(k):
        return s + 2 * (lax.rem(zi + k + 8, 8) - zi)

    core_twin = s + 1 - 2 * lax.rem(s, 2)
    peers = [(s, slab_at(k)) for k in (-2, -1, 1, 2)] + [(z_at(k), b) for k in (-2, -1, 1, 2)]
    peers += [(core_twin, b), (shot_at(16), b)]

    def tell(token, others):
        for other in others:
            pl.semaphore_signal(token, inc=1, device_id=other, device_id_type=MESH)

    for peer in peers:
        pl.semaphore_signal(barrier, inc=1, device_id=peer, device_id_type=MESH)

    loads = [pltpu.make_async_copy(hbm[at], loaded[at], load_s.at[at]) for at in range(12)]
    for at in (4, 1, 0, 3, 2, 5, 6, 7, 8, 9, 10, 11):
        loads[at].start()
    loads[4].wait()
    sv[...] = (vel[...] - MID).astype(BF16)
    for at in (0, 1, 2, 3):
        loads[at].wait()
    pl.semaphore_wait(barrier, len(peers))
    tell(token_slab2, [(s, slab_at(-2)), (s, slab_at(2))])
    tell(token_z, [(z_at(-2), b), (z_at(2), b)])

    sent = []
    first = ([], [])

    def send_first(f):
        now, old = ((cur, prev), (acur, anext))[f]
        for side, step in ((0, 1), (1, -1)):
            target = slab_at(step)
            edge = pl.ds(4, 4) if step == 1 else pl.ds(0, 4)
            at = init_s.at[side, 2 * f], init_r.at[side, 2 * f]
            first[f].append(send(now.at[0], rc.at[side, f], *at, s, target))
            at = init_s.at[side, 2 * f + 1], init_r.at[side, 2 * f + 1]
            first[f].append(send(old.at[0, edge], rp.at[side, f], *at, s, target))
            if f == 0:
                first[f].append(send(sv.at[edge], rn.at[side], init_s.at[side, 4], init_r.at[side, 4], s, target))

    send_first(0)

    for at in range(5, 12):
        loads[at].wait()
    lane = lax.broadcasted_iota(jnp.int32, (64, 128), 1)
    diff = jnp.abs(lax.broadcasted_iota(jnp.int32, (128, 128), 0) - lax.broadcasted_iota(jnp.int32, (128, 128), 1))
    band = jnp.where(diff == 0, 3.0 * COEFFS[0], 0.0)
    for m in range(1, 5):
        band = jnp.where(diff == m, COEFFS[m], band)
    band_h, band_l = split(band, 2)
    bands[0:128, :] = band_h
    bands[128:256, :] = band_h
    bandl[...] = band_l

    for ref in (u0, u1, wa0, wa1, da, db):
        ref[:, 0:TOP, :] = jnp.zeros((ref.shape[0], TOP, 128), F32)
        ref[:, TOP + ROWS:, :] = jnp.zeros((ref.shape[0], 8, 128), F32)
    db[:, YS, :] = jnp.zeros((db.shape[0], ROWS, 128), F32)
    u0[8:16, YS, :] = cur[0].astype(F32)
    u1[8:16, YS, :] = acur[0].astype(F32)
    wa0[8:16, YS, :] = prev[0].astype(F32)
    wa1[8:16, YS, :] = anext[0].astype(F32)
    scaled = vel[...] * COURANT
    kap[16:24] = scaled * scaled

    cells = rec[...]
    rec_row = lax.shift_right_logical(cells, 7)
    rec_lane = cells & 127
    sub = lax.broadcasted_iota(jnp.int32, (8, 256), 0)
    digits = jnp.where(sub == 0, lax.shift_right_logical(rec_row, 6),
                       jnp.where(sub == 1, rec_row & 63, jnp.where(sub == 2, rec_lane, 0)))
    eye = jnp.where(
        lax.broadcasted_iota(jnp.int32, (256, 256), 0) == lax.broadcasted_iota(jnp.int32, (256, 256), 1),
        1.0, 0.0).astype(BF16)
    columns = lax.dot_general(eye, digits.astype(F32).astype(BF16), NT, preferred_element_type=F32)
    row_col = columns[:, 0:1] * 64.0 + columns[:, 1:2] - (b * 256).astype(F32)
    lane_col = columns[:, 2:3]
    lane_hot[...] = jnp.where(lane_col == lax.broadcasted_iota(jnp.int32, (256, 128), 1).astype(F32), 1.0, 0.0)
    pick[...] = jnp.where(
        row_col == lax.broadcasted_iota(jnp.int32, (256, 256), 1).astype(F32), 1.0, 0.0).astype(BF16)
    relative = rec_row - (b * 256 - 20 * ROWS)
    for q in range(6):
        hot[256 * q:256 * q + 256, :] = jnp.where(
            lax.broadcasted_iota(jnp.int32, (256, 256), 0) + 256 * q == relative, 1.0, 0.0).astype(BF16)
    cell = src[0]
    src_plane = lax.shift_right_logical(cell, 12)
    src_row = lax.shift_right_logical(cell, 7) & 31
    src_lane = cell & 127
    src_hot[...] = jnp.where(
        (lax.broadcasted_iota(jnp.int32, (ROWS, 128), 0) == src_row)
        & (lax.broadcasted_iota(jnp.int32, (ROWS, 128), 1) == src_lane), 1.0, 0.0)

    def iota(rows, columns, axis):
        return lax.broadcasted_iota(jnp.int32, (rows, columns), axis)

    def one_hot(condition):
        return jnp.where(condition, 1.0, 0.0).astype(BF16)

    eye64 = one_hot(iota(64, 64, 0) == iota(64, 64, 1))
    wf[...] = jnp.zeros((96, 64), F32)
    for t in range(27):
        wf[2 * t:2 * t + 2, :] = wi[t].astype(F32)
    wf[64:91, :] = wo[...].astype(F32)
    taps_in = wf[0:64, :].astype(BF16)
    taps_out = wf[64:96, :].astype(BF16)
    q = iota(96, 64, 0)
    i, j, c = (q >> 3) & 3, (q >> 1) & 3, q & 1
    wanted = one_hot((iota(96, 64, 1) == (9 * i + 3 * j + (q >> 5)) * 2 + c) & (i < 3) & (j < 3))
    chosen = dot(wanted, taps_in).astype(BF16)
    w1[...] = lax.dot_general(eye64, chosen, NT, preferred_element_type=F32).astype(BF16)
    for k in range(3):
        for u in range(0, 9, 2):
            blocks = [wd[9 * (v % 3) + 3 * (v // 3) + k] for v in range(u, min(u + 2, 9))]
            both = lax.dot_general(eye64, jnp.concatenate(blocks, axis=0), NT, preferred_element_type=F32)
            wm[64 * k:64 * k + 64, 64 * u:64 * (u + len(blocks))] = both.astype(BF16)
    for u in range(0, 9, 2):
        both = jnp.zeros((16, 128), F32)
        for v in range(u, min(u + 2, 9)):
            wanted = one_hot((iota(16, 32, 1) == 9 * (v % 3) + 3 * (v // 3) + iota(16, 32, 0)) & (iota(16, 32, 0) < 3))
            place = one_hot(iota(64, 128, 1) == iota(64, 128, 0) + 64 * (v - u))
            both = both + dot(dot(wanted, taps_out).astype(BF16), place)
        w3[:, 64 * u:min(64 * u + 128, 576)] = both[:, 0:min(128, 576 - 64 * u)].astype(BF16)
    sub64 = iota(8, 64, 0)
    biases = jnp.zeros((8, 64), F32)
    for at, part in enumerate(split(bi[...], 3) + split(bd[...], 3)):
        biases = jnp.where(sub64 == at, part.astype(F32), biases)
    bias_col = lax.dot_general(eye64, biases.astype(BF16), NT, preferred_element_type=F32)
    b1 = bias_col[:, 0:1] + bias_col[:, 1:2] + bias_col[:, 2:3]
    b2 = bias_col[:, 3:4] + bias_col[:, 4:5] + bias_col[:, 5:6]
    r, col = iota(384, 144, 0), iota(384, 144, 1)
    group = jnp.where(col >= 48, 1, 0) + jnp.where(col >= 96, 1, 0)
    rest = col - 48 * group
    part_of = rest >> 4
    widen[...] = one_hot(
        (((r >> 1) & 3) == group) & ((r & 1) == ((rest >> 3) & 1)) & (((r >> 3) & 3) < 3)
        & (8 * part_of + (rest & 7) == (r >> 5) + ((r >> 3) & 3) + 5))

    send_first(1)
    for slot, step in enumerate((2, 1, -1, -2)):
        send(sv.at[zi], vp.at[slot], vp_s, vp_r, s, slab_at(step))
    sent += first[0] + first[1]

    def z_pass(field, lo, n):
        for c in range(n // 8):
            x = field[lo + 8 * c:lo + 8 * c + 8, YS, :].reshape(256, 128)
            hi, low = split(x, 2)
            z = dot(jnp.concatenate([hi, low], axis=1), bands[...]) + dot(hi, bandl[...])
            zs[8 * c:8 * c + 8] = z.reshape(8, ROWS, 128)

    def advance(field, old, lo, n, kap_lo, extra):
        def four(g, carry):
            i0 = 4 * g
            j0 = lo + i0
            for q in range(ROWS // 8):
                rows = slice(8 * q, 8 * q + 8)
                window = [field[j0 + k - 4, TOP + 8 * q:TOP + 8 * q + 8, :] for k in range(12)]
                for p in range(4):
                    acc = zs[i0 + p, rows, :]
                    for m in range(1, 5):
                        at = TOP + 8 * q
                        around = (window[p + 4 + m] + window[p + 4 - m]) + (
                            field[j0 + p, at + m:at + m + 8, :] + field[j0 + p, at - m:at - m + 8, :])
                        acc = acc + COEFFS[m] * around
                    ys = slice(TOP + 8 * q, TOP + 8 * q + 8)
                    new = 2.0 * window[p + 4] - old[j0 + p, ys, :] + kap[kap_lo + i0 + p, rows, :] * acc
                    old[j0 + p, ys, :] = extra(i0 + p, j0 + p, rows, new, acc)
            return carry
        lax.fori_loop(0, n // 4, four, 0)

    def plain(i, j, rows, new, acc):
        return new

    def forward_extra(n):
        weight = wav[0, n]
        first_plane = b * 8 - 8

        def extra(i, j, rows, new, acc):
            zs[i, rows, :] = acc
            amount = jnp.where(src_plane == first_plane + j, weight, 0.0)
            return new + src_hot[rows, :] * amount
        return extra

    def sample(field, n):
        x = field[8:16, YS, :].reshape(256, 128)
        g = dot(pick[...], jnp.concatenate(split(x, 3), axis=1))
        hot3 = jnp.concatenate([lane_hot[...]] * 3, axis=1)
        values = lax.dot_general(jnp.ones((8, 384), BF16), (g * hot3).astype(BF16), NT, preferred_element_type=F32)
        tr[n:n + 1, :] = values[0:1, :]

    tr[...] = jnp.zeros((8, 256), F32)
    left, right = inside(-1), inside(1)

    def kappa_of(values, valid):
        value = (values.astype(F32) + MID) * COURANT
        return value * value * valid

    def fill(now, from_left, from_right):
        now[0:8, YS, :] = from_left.astype(F32) * left
        now[16:24, YS, :] = from_right.astype(F32) * right

    fields = ((u0, wa0), (u1, wa1))
    copies = [None, None]

    def round_of(r, f):
        now, old = fields[f]
        if r == 0:
            for copy in first[f]:
                copy.wait_recv()
            fill(now, rc[0, f], rc[1, f])
            old[4:8, YS, :] = rp[0, f].astype(F32) * left
            old[16:20, YS, :] = rp[1, f].astype(F32) * right
            if f == 0:
                kap[12:16] = kappa_of(rn[0], left)
                kap[24:28] = kappa_of(rn[1], right)
        else:
            for copy in copies[f]:
                copy.wait_recv()
            fill(now, rb[r - 1, f, 0], rb[r - 1, f, 1])
        n = 2 * r
        z_pass(now, 4, 16)
        advance(now, old, 4, 16, 12, plain if f else forward_extra(n))
        if f == 0:
            lap[n] = zs[4:12]
        z_pass(old, 8, 8)
        advance(old, now, 8, 8, 16, plain if f else forward_extra(n + 1))
        if f == 0:
            lap[n + 1] = zs[0:8]
        if r < 2:
            sb[r, f] = now[8:16, YS, :].astype(BF16)
            copies[f] = [
                send(sb.at[r, f], rb.at[r, f, side], round_s.at[2 * r + f, side], round_r.at[2 * r + f, side],
                     s, slab_at(step))
                for side, step in ((0, 1), (1, -1))]
            sent.extend(copies[f])
        if f == 0:
            sample(old, n)
            sample(now, n + 1)
        else:
            hom[STEPS - 1 - n] = old[8:16, YS, :]
            hom[STEPS - 2 - n] = now[8:16, YS, :]

    round_of(0, 0)
    pl.semaphore_wait(token_slab2, 2)
    tell(token_slab4, [(s, slab_at(-4)), (s, slab_at(4))])
    pl.semaphore_wait(token_z, 2)
    tell(token_core, [(core_twin, b)])
    pltpu.make_async_copy(vp, vp, vp_r).wait()
    for k in range(1, 8):
        send(vp, rv.at[k - 1], rv_s, rv_r, z_at(k), b)
    round_of(0, 1)
    round_of(1, 0)
    pl.semaphore_wait(token_slab4, 2)
    pl.semaphore_wait(token_core, 1)
    tell(token_half, [(shot_at(16), b)])
    round_of(1, 1)
    round_of(2, 0)
    pl.semaphore_wait(token_half, 1)
    tell(token_beside, [(s, slab_at(-1)), (s, slab_at(1))])

    for k in range(1, slabs):
        send(tr, rt.at[k - 1], tr_s, tr_r, s, slab_at(k))
    round_of(2, 1)
    image = hom[0] * lap[0]
    for n in range(1, STEPS):
        image = image + hom[n] * lap[n]
    img[...] = image
    pltpu.make_async_copy(rv, rv, rv_r).wait()
    near_far = ((0, inside(-2)), (8, left), (24, right), (32, inside(2)))
    for k in range(8):
        plane = lax.rem(zi - k + 8, 8)
        for slot, (base, valid) in enumerate(near_far):
            kap[base + plane] = kappa_of(rv[k - 1, slot] if k else vp[slot], valid)
    pltpu.make_async_copy(rt, rt, tr_r).wait()
    total = tr[...]
    for k in range(slabs - 1):
        total = total + rt[k]
    mf[...] = jnp.zeros((8, 256), F32)
    for n in range(STEPS):
        trace = total[n:n + 1] - obs[n]
        mis[n] = trace
        mf[n:n + 1, :] = trace
    amounts = jnp.zeros((256, 8), F32)
    for part in split(mf[...], 3):
        amounts = amounts + lax.dot_general(eye, part, NT, preferred_element_type=F32)

    def inject(n, plane, planes):
        parts = split(amounts[:, n:n + 1] * lane_hot[...], 2)
        rhs = jnp.concatenate(parts, axis=1)
        for c in range(planes // 8):
            start = (plane + 8 * c) * ROWS
            both = dot(hot[start:start + 256, :], rhs)
            yield c, (both[:, 0:128] + both[:, 128:256]).reshape(8, ROWS, 128)

    for c, values in inject(5, 0, 48):
        da[8 * c:8 * c + 8, YS, :] = values
    img[...] += da[20:28, YS, :] * lap[5]

    def with_misfit(i, j, rows, new, acc):
        return new + js[i, rows, :]

    near, old = da, db
    for n in range(4, -1, -1):
        reach = 4 * n
        lo, planes = 20 - reach, 8 + 2 * reach
        z_pass(near, lo, planes)
        for c, values in inject(n, lo, planes):
            js[8 * c:8 * c + 8] = values
        advance(near, old, lo, planes, lo - 4, with_misfit)
        near, old = old, near
        img[...] += near[20:28, YS, :] * lap[n]

    by_row = jnp.swapaxes(img[...], 0, 1).reshape(8, 2, 16, 128)
    for core in range(2):
        imgt[core] = by_row[:, core]
    core = lax.rem(s, 2)
    chip = lax.div(s, 2)
    chips = shots // 2
    swap = send(imgt.at[1 - core], ip, ip_s, ip_r, core_twin, b)
    sent.append(swap)
    swap.wait_recv()
    chip_sum[...] = imgt[core] + ip[...]
    for k in range(1, chips):
        target = lax.rem(chip + k, chips)
        send(chip_sum.at[lax.rem(target, 8)], ri.at[chip], im_s, im_r, 2 * target + core, b)
    ri[chip] = chip_sum[zi]
    row_of = lax.broadcasted_iota(jnp.int32, (8, ROWS, 128), 1)
    own_velocity = jnp.concatenate(
        [jnp.sum(jnp.where(row_of == 2 * pair + y, vel[...], 0.0), axis=1) for y in range(2)], axis=0)
    pl.semaphore_wait(token_beside, 2)
    pltpu.make_async_copy(ri.at[0:chips - 1], ri.at[0:chips - 1], im_r).wait()
    summed = ri[0]
    for k in range(1, chips):
        summed = summed + ri[k]
    update = RATE * (summed / shots)
    moved = own_velocity - update
    centered = moved - CENTER
    for y in range(2):
        fs[y] = jnp.concatenate([centered[8 * y:8 * y + 8], update[8 * y:8 * y + 8]], axis=0).astype(BF16)

    for slot, (dx, dr) in enumerate(cross):
        send(fs, rf.at[slot], ft_s, ft_r, half + lax.rem(pair - dr + 16, 16), slab_at(-dx))
    pltpu.make_async_copy(rf, rf, ft_r).wait()
    lane16 = iota(16, 128, 1)

    def place_features(at, values):
        feat[at, :, 0:128] = jnp.where(lane16 == 0, 0.0, pltpu.roll(values, 1, 1)).astype(BF16)
        feat[at, :, 128:256] = values.astype(BF16)
        feat[at, :, 256:384] = jnp.where(lane16 == 127, 0.0, pltpu.roll(values, 127, 1)).astype(BF16)

    def row_inside(k):
        return jnp.where((2 * pair + k >= 0) & (2 * pair + k < ROWS), 1.0, 0.0).astype(F32)

    for slot, (dx, dr) in enumerate(cross):
        valid = inside(dx) * row_inside(2 * dr)
        for y in range(2):
            place_features((2 * dr + 4 + y) * 3 + dx + 1, rf[slot, y].astype(F32) * valid)
    for y in range(2):
        place_features((4 + y) * 3 + 1, fs[y].astype(F32))

    def first_conv(y, carry):
        spread = dot(widen[...], feat[pl.ds(3 * y + 3, 9)].reshape(144, 384)).astype(BF16)
        for k in range(3):
            im[:, k] = spread[:, 128 * k:128 * k + 128].reshape(12, 32, 128)
        row_ok = row_inside(y - 2)
        for x0 in range(0, 12, 2):
            g = dot(w1[...], jnp.concatenate([im[x0].reshape(96, 128), im[x0 + 1].reshape(96, 128)], axis=1))
            for half in range(2):
                plane = b * 8 + x0 + half - 2
                ok = jnp.where((plane >= 0) & (plane < slabs * 8), row_ok, 0.0)
                value = jnp.maximum(g[:, 128 * half:128 * half + 128] + b1, 0.0) * ok
                h1[y, x0 + half] = value.astype(BF16)
        return carry

    lax.fori_loop(0, 6, first_conv, 0)

    def second_conv(y, carry):
        row_ok = row_inside(y - 1)
        for x0 in range(0, 10, 2):
            halves = []
            for x in (x0, x0 + 1):
                halves.append(jnp.concatenate([h1[y + j, x:x + 3].reshape(192, 128) for j in range(3)], axis=0))
            g = dot(wm[...], jnp.concatenate(halves, axis=1))
            for half in range(2):
                x = x0 + half
                plane = b * 8 + x - 1
                ok = jnp.where((plane >= 0) & (plane < slabs * 8), row_ok, 0.0)
                value = jnp.maximum(z_combine(g[:, 128 * half:128 * half + 128], lane) + b2, 0.0) * ok
                h2[y, x] = value.astype(BF16)
        return carry

    lax.fori_loop(0, 4, second_conv, 0)

    lane1 = lax.broadcasted_iota(jnp.int32, (1, 128), 1)
    for y in range(2):
        for x in range(0, 8, 2):
            halves = []
            for at in (x, x + 1):
                halves.append(jnp.concatenate([h2[y + j, at:at + 3].reshape(192, 128) for j in range(3)], axis=0))
            pair_g = dot(w3[...], jnp.concatenate(halves, axis=1))
            for at in range(2):
                g = pair_g[0:8, 128 * at:128 * at + 128]
                low = jnp.where(lane1 == 0, 0.0, pltpu.roll(g, 1, 1)[0:1])
                high = jnp.where(lane1 == 127, 0.0, pltpu.roll(g, 127, 1)[2:3])
                i = 8 * y + x + at
                row[i:i + 1, :] = moved[i:i + 1] + (g[1:2] + low + high + b3[0])

    for k in range(1, 16):
        send(row, ro.at[k - 1], ou_s, ou_r, half + lax.rem(pair + k, 16), b)
    out[pair] = row[...]
    pltpu.make_async_copy(ro, ro, ou_r).wait()
    for k in range(1, 16):
        out[lax.rem(pair - k + 16, 16)] = ro[k - 1]

    for copy in sent:
        copy.wait_send()
    pltpu.make_async_copy(vp, vp, vp_s).wait()
    pltpu.make_async_copy(rv, rv, rv_s).wait()
    pltpu.make_async_copy(rt, rt, tr_s).wait()
    pltpu.make_async_copy(ri.at[0:chips - 1], ri.at[0:chips - 1], im_s).wait()
    pltpu.make_async_copy(rf, rf, ft_s).wait()
    pltpu.make_async_copy(ro, ro, ou_s).wait()


def shards(slabs, shots, previous_field, current_field, adjoint_next, adjoint_current, velocity, wavelet, source_cell,
           receiver_cell, observed, weight_in, bias_in, weight_mid, bias_mid, weight_out, bias_out):
    vmem = pl.BlockSpec(memory_space=pltpu.VMEM)
    smem = pl.BlockSpec(memory_space=pltpu.SMEM)
    f32 = lambda *shape: pltpu.VMEM(shape, F32)
    bf = lambda *shape: pltpu.VMEM(shape, BF16)
    dma = pltpu.SemaphoreType.DMA
    arrays = (previous_field, current_field, adjoint_next, adjoint_current, velocity, receiver_cell,
              jnp.swapaxes(observed, 0, 1), weight_in, bias_in[None], weight_mid, bias_mid[None], weight_out.reshape(27, 64))
    scratch = [pltpu.VMEM(a.shape, a.dtype) for a in arrays] + [
        f32(24, 48, 128), f32(24, 48, 128), f32(24, 48, 128), f32(24, 48, 128),
        f32(48, 48, 128), f32(48, 48, 128), f32(40, 32, 128), f32(40, 32, 128), f32(40, 32, 128),
        f32(6, 8, 32, 128), f32(6, 8, 32, 128), f32(8, 32, 128), f32(2, 8, 16, 128), f32(8, 16, 128), f32(8, 16, 128),
        bf(8, 32, 128), bf(4, 32, 128), bf(7, 4, 32, 128), bf(2, 4, 32, 128), bf(2, 2, 8, 32, 128), bf(2, 2, 4, 32, 128),
        bf(2, 2, 8, 32, 128), bf(2, 2, 2, 8, 32, 128),
        f32(8, 256), f32(slabs - 1, 8, 256), f32(8, 256),
        bf(1536, 256), bf(256, 256), f32(256, 128), f32(32, 128), bf(256, 128), bf(128, 128),
        f32(shots // 2, 16, 128), bf(2, 16, 128), bf(14, 2, 16, 128), bf(30, 16, 384),
        f32(96, 64), bf(64, 96), bf(192, 576), bf(16, 576), bf(384, 144), bf(12, 3, 32, 128),
        bf(6, 12, 64, 128), bf(4, 10, 64, 128), f32(16, 128), f32(15, 16, 128),
        dma((2, 5)), dma((2, 5)), dma, dma, dma, dma, dma((4, 2)), dma((4, 2)),
    ] + [dma] * 8 + [dma((12,)), dma, dma] + [pltpu.SemaphoreType.REGULAR] * 6
    rows, misfit = pl.pallas_call(
        functools.partial(kernel, slabs, shots),
        out_shape=(jax.ShapeDtypeStruct((16, 16, 128), F32), jax.ShapeDtypeStruct((STEPS, 1, 256), F32)),
        in_specs=[smem, smem, smem] + [pl.BlockSpec(memory_space=pl.ANY)] * 12,
        out_specs=(vmem, vmem),
        scratch_shapes=scratch,
        compiler_params=pltpu.CompilerParams(
            collective_id=0, has_side_effects=True, vmem_limit_bytes=60 * 1024 * 1024),
    )(wavelet, source_cell, bias_out, *arrays)
    return jnp.swapaxes(rows.reshape(ROWS, 8, 128), 0, 1), jnp.swapaxes(misfit, 0, 1)


def solution(mesh):
    placed = (
        P("shot", "slab", None, None), P("shot", "slab", None, None), P("shot", "slab", None, None),
        P("shot", "slab", None, None), P("slab", None, None), P("shot", None), P("shot"), P("shot", None),
        P("shot", None, None), P(), P(), P(), P(), P(), P(),
    )
    return jax.shard_map(
        functools.partial(shards, mesh.shape["slab"], mesh.shape["shot"]),
        mesh=mesh,
        in_specs=placed,
        out_specs=(P("slab", None, None), P("shot", None, None)),
        check_vma=False,
    )
```

```python
import functools

import jax
import jax.numpy as jnp
from jax import lax
from jax.experimental import pallas as pl
from jax.experimental.pallas import tpu as pltpu
from jax.sharding import PartitionSpec as P

COEFFS = (-205.0 / 72.0, 8.0 / 5.0, -1.0 / 5.0, 8.0 / 315.0, -1.0 / 560.0)
COURANT = 0.1
RATE = 0.2
CENTER = 3.0
MID = 2.75
MESH = pl.DeviceIdType.MESH
F32 = jnp.float32
BF16 = jnp.bfloat16
NT = (((1,), (1,)), ((), ()))
STEPS = 6
TOP, ROWS = 8, 32
YS = slice(TOP, TOP + ROWS)


def dot(a, b):
    return jnp.dot(a, b, preferred_element_type=F32)


def split(x, pieces):
    parts = []
    for _ in range(pieces):
        part = x.astype(BF16)
        parts.append(part)
        x = x - part.astype(F32)
    return parts


def z_combine(g, lane):
    low = jnp.where(lane == 0, 0.0, pltpu.roll(g[0:64], 1, 1))
    high = jnp.where(lane == 127, 0.0, pltpu.roll(g[128:192], 127, 1))
    return g[64:128] + low + high


def kernel(
    slabs, shots,
    wav, src, b3, *refs,
):
    hbm, (out, mis), loaded, rest = refs[:12], refs[12:14], refs[14:26], refs[26:]
    prev, cur, anext, acur, vel, rec, obs, wi, bi, wd, bd, wo = loaded
    (
        u0, u1, wa0, wa1, da, db, zs, js, kap, lap, hom, img, imgt, ip, chip_sum, sv, vp, rv, rn, rc, rp, sb, rb, tr, rt, rl, mf, hot, pick, lane_hot, src_hot, bands, bandl, ri, fs, fe, rf, re, feat, wf, w1, wm, w3, band1, h1, h2, row, ro, by_owner, init_s, init_r, vp_s, vp_r, rv_s, rv_r, round_s, round_r, tr_s, tr_r, im_s, im_r, ft_s, ft_r, ou_s, ou_r, load_s, ip_s, ip_r, rl_s, rl_r, fe_s, fe_r,
        token_slab2, token_slab4, token_z, token_core, token_half, token_beside,
    ) = rest
    s = lax.axis_index("shot")
    b = lax.axis_index("slab")

    def shot_at(k):
        return lax.rem(s + k + shots, shots)

    def slab_at(k):
        return lax.rem(b + k + slabs, slabs)

    def inside(k):
        return jnp.where((b + k >= 0) & (b + k < slabs), 1.0, 0.0).astype(F32)

    def send(source, target, ss, rs, shot, slab):
        copy = pltpu.make_async_remote_copy(
            src_ref=source, dst_ref=target, send_sem=ss, recv_sem=rs,
            device_id=(shot, slab), device_id_type=MESH)
        copy.start()
        return copy

    barrier = pltpu.get_barrier_semaphore()
    zi = lax.rem(lax.div(s, 2), 8)
    pair = lax.rem(s, 16)
    half = s - pair

    def z_at(k):
        return s + 2 * (lax.rem(zi + k + 8, 8) - zi)

    core_twin = s + 1 - 2 * lax.rem(s, 2)
    peers = [(s, slab_at(k)) for k in (-2, -1, 1, 2)] + [(z_at(k), b) for k in (-2, -1, 1, 2)]
    peers += [(core_twin, b), (shot_at(16), b)]

    def tell(token, others):
        for other in others:
            pl.semaphore_signal(token, inc=1, device_id=other, device_id_type=MESH)

    for peer in peers:
        pl.semaphore_signal(barrier, inc=1, device_id=peer, device_id_type=MESH)

    loads = [pltpu.make_async_copy(hbm[at], loaded[at], load_s.at[at]) for at in range(12)]
    for at in (4, 1, 0, 3, 2, 5, 6, 7, 8, 9, 10, 11):
        loads[at].start()
    pl.semaphore_wait(barrier, len(peers))
    tell(token_slab2, [(s, slab_at(-2)), (s, slab_at(2))])
    tell(token_z, [(z_at(-2), b), (z_at(2), b)])

    sent = []
    first = ([], [])

    def send_first(f):
        now, old = ((hbm[1], hbm[0]), (acur, anext))[f]
        for side, step in ((0, 1), (1, -1)):
            target = slab_at(step)
            edge = pl.ds(4, 4) if step == 1 else pl.ds(0, 4)
            at = init_s.at[side, 2 * f], init_r.at[side, 2 * f]
            first[f].append(send(now.at[0], rc.at[side, f], *at, s, target))
            at = init_s.at[side, 2 * f + 1], init_r.at[side, 2 * f + 1]
            first[f].append(send(old.at[0, edge], rp.at[side, f], *at, s, target))
        for side, step in ((0, 1), (1, -1)) if f == 0 else ():
            if side == 0:
                loads[4].wait()
                sv[...] = (vel[...] - MID).astype(BF16)
            edge = pl.ds(4, 4) if step == 1 else pl.ds(0, 4)
            first[f].append(send(sv.at[edge], rn.at[side], init_s.at[side, 4], init_r.at[side, 4], s, slab_at(step)))

    send_first(0)

    for at in (0, 1, 2, 3, *range(5, 12)):
        loads[at].wait()
    lane = lax.broadcasted_iota(jnp.int32, (64, 128), 1)
    diff = jnp.abs(lax.broadcasted_iota(jnp.int32, (128, 128), 0) - lax.broadcasted_iota(jnp.int32, (128, 128), 1))
    band = jnp.where(diff == 0, 3.0 * COEFFS[0], 0.0)
    for m in range(1, 5):
        band = jnp.where(diff == m, COEFFS[m], band)
    band_h, band_l = split(band, 2)
    bands[0:128, :] = band_h
    bands[128:256, :] = band_h
    bandl[...] = band_l

    for ref in (u0, u1, wa0, wa1, da, db):
        ref[:, 0:TOP, :] = jnp.zeros((ref.shape[0], TOP, 128), F32)
        ref[:, TOP + ROWS:, :] = jnp.zeros((ref.shape[0], 8, 128), F32)
    db[:, YS, :] = jnp.zeros((db.shape[0], ROWS, 128), F32)
    u0[8:16, YS, :] = cur[0].astype(F32)
    u1[8:16, YS, :] = acur[0].astype(F32)
    wa0[8:16, YS, :] = prev[0].astype(F32)
    wa1[8:16, YS, :] = anext[0].astype(F32)
    scaled = vel[...] * COURANT
    kap[16:24] = scaled * scaled

    cells = rec[...]
    rec_row = lax.shift_right_logical(cells, 7)
    rec_lane = cells & 127
    sub = lax.broadcasted_iota(jnp.int32, (8, 256), 0)
    digits = jnp.where(sub == 0, lax.shift_right_logical(rec_row, 6),
                       jnp.where(sub == 1, rec_row & 63, jnp.where(sub == 2, rec_lane, 0)))
    eye = jnp.where(
        lax.broadcasted_iota(jnp.int32, (256, 256), 0) == lax.broadcasted_iota(jnp.int32, (256, 256), 1),
        1.0, 0.0).astype(BF16)
    columns = lax.dot_general(eye, digits.astype(F32).astype(BF16), NT, preferred_element_type=F32)
    row_col = columns[:, 0:1] * 64.0 + columns[:, 1:2] - (b * 256).astype(F32)
    lane_col = columns[:, 2:3]
    lane_hot[...] = jnp.where(lane_col == lax.broadcasted_iota(jnp.int32, (256, 128), 1).astype(F32), 1.0, 0.0)
    pick[...] = jnp.where(
        row_col == lax.broadcasted_iota(jnp.int32, (256, 256), 1).astype(F32), 1.0, 0.0).astype(BF16)
    relative = rec_row - (b * 256 - 20 * ROWS)
    for q in range(6):
        hot[256 * q:256 * q + 256, :] = jnp.where(
            lax.broadcasted_iota(jnp.int32, (256, 256), 0) + 256 * q == relative, 1.0, 0.0).astype(BF16)
    cell = src[0]
    src_plane = lax.shift_right_logical(cell, 12)
    src_row = lax.shift_right_logical(cell, 7) & 31
    src_lane = cell & 127
    src_hot[...] = jnp.where(
        (lax.broadcasted_iota(jnp.int32, (ROWS, 128), 0) == src_row)
        & (lax.broadcasted_iota(jnp.int32, (ROWS, 128), 1) == src_lane), 1.0, 0.0)

    def iota(rows, columns, axis):
        return lax.broadcasted_iota(jnp.int32, (rows, columns), axis)

    def one_hot(condition):
        return jnp.where(condition, 1.0, 0.0).astype(BF16)

    eye64 = one_hot(iota(64, 64, 0) == iota(64, 64, 1))
    wf[...] = jnp.zeros((96, 64), F32)
    for t in range(27):
        wf[2 * t:2 * t + 2, :] = wi[t].astype(F32)
    wf[64:91, :] = wo[...].astype(F32)
    taps_in = wf[0:64, :].astype(BF16)
    taps_out = wf[64:96, :].astype(BF16)
    q = iota(96, 64, 0)
    i, j, c = (q >> 3) & 3, (q >> 1) & 3, q & 1
    wanted = one_hot((iota(96, 64, 1) == (9 * i + 3 * j + (q >> 5)) * 2 + c) & (i < 3) & (j < 3))
    chosen = dot(wanted, taps_in).astype(BF16)
    for k in range(3):
        w1[64 * k:64 * k + 64, :] = lax.dot_general(
            eye64, chosen[32 * k:32 * k + 32], NT, preferred_element_type=F32).astype(BF16)
    for k in range(3):
        for u in range(0, 9, 2):
            blocks = [wd[9 * (v % 3) + 3 * (v // 3) + k] for v in range(u, min(u + 2, 9))]
            both = lax.dot_general(eye64, jnp.concatenate(blocks, axis=0), NT, preferred_element_type=F32)
            wm[64 * k:64 * k + 64, 64 * u:64 * (u + len(blocks))] = both.astype(BF16)
    for u in range(0, 9, 2):
        both = jnp.zeros((16, 128), F32)
        for v in range(u, min(u + 2, 9)):
            wanted = one_hot((iota(16, 32, 1) == 9 * (v % 3) + 3 * (v // 3) + iota(16, 32, 0)) & (iota(16, 32, 0) < 3))
            place = one_hot(iota(64, 128, 1) == iota(64, 128, 0) + 64 * (v - u))
            both = both + dot(dot(wanted, taps_out).astype(BF16), place)
        w3[:, 64 * u:min(64 * u + 128, 576)] = both[:, 0:min(128, 576 - 64 * u)].astype(BF16)
    sub64 = iota(8, 64, 0)
    biases = jnp.zeros((8, 64), F32)
    for at, part in enumerate(split(bi[...], 3) + split(bd[...], 3)):
        biases = jnp.where(sub64 == at, part.astype(F32), biases)
    bias_col = lax.dot_general(eye64, biases.astype(BF16), NT, preferred_element_type=F32)
    b1 = bias_col[:, 0:1] + bias_col[:, 1:2] + bias_col[:, 2:3]
    b2 = bias_col[:, 3:4] + bias_col[:, 4:5] + bias_col[:, 5:6]
    r, col = iota(32, 96, 0), iota(32, 96, 1)
    group = jnp.where(col >= 32, 1, 0) + jnp.where(col >= 64, 1, 0)
    rest = col - 32 * group
    before, after = rest < 8, rest >= 24
    edge_rest = jnp.where(after, rest - 24, rest)
    channel = jnp.where(before | after, edge_rest >> 2, (rest - 8) >> 3)
    plane_of = jnp.where(before, edge_rest & 3, jnp.where(after, 12 + (edge_rest & 3), 4 + ((rest - 8) & 7)))
    fits = (((r >> 1) & 3) == group) & ((r & 1) == channel) & ((r >> 3) < 3)
    shift = plane_of - (r >> 3) - 1
    for x in range(12):
        wide = dot(w1[...], one_hot(fits & (shift == x))).astype(BF16)
        for k in range(3):
            band1[k, 64 * x:64 * x + 64, :] = wide[64 * k:64 * k + 64]

    send_first(1)
    for slot, step in enumerate((2, 1, -1, -2)):
        send(sv.at[zi], vp.at[slot], vp_s, vp_r, s, slab_at(step))
    sent += first[0] + first[1]

    def z_pass(field, lo, n):
        for c in range(n // 8):
            x = field[lo + 8 * c:lo + 8 * c + 8, YS, :].reshape(256, 128)
            hi, low = split(x, 2)
            z = dot(jnp.concatenate([hi, low], axis=1), bands[...]) + dot(hi, bandl[...])
            zs[8 * c:8 * c + 8] = z.reshape(8, ROWS, 128)

    def advance(field, old, lo, n, kap_lo, extra):
        def four(g, carry):
            i0 = 4 * g
            j0 = lo + i0
            for q in range(ROWS // 8):
                rows = slice(8 * q, 8 * q + 8)
                window = [field[j0 + k - 4, TOP + 8 * q:TOP + 8 * q + 8, :] for k in range(12)]
                for p in range(4):
                    acc = zs[i0 + p, rows, :]
                    for m in range(1, 5):
                        at = TOP + 8 * q
                        around = (window[p + 4 + m] + window[p + 4 - m]) + (
                            field[j0 + p, at + m:at + m + 8, :] + field[j0 + p, at - m:at - m + 8, :])
                        acc = acc + COEFFS[m] * around
                    ys = slice(TOP + 8 * q, TOP + 8 * q + 8)
                    new = 2.0 * window[p + 4] - old[j0 + p, ys, :] + kap[kap_lo + i0 + p, rows, :] * acc
                    old[j0 + p, ys, :] = extra(i0 + p, j0 + p, rows, new, acc)
            return carry
        lax.fori_loop(0, n // 4, four, 0)

    def plain(i, j, rows, new, acc):
        return new

    def forward_extra(n):
        weight = wav[0, n]
        first_plane = b * 8 - 8

        def extra(i, j, rows, new, acc):
            zs[i, rows, :] = acc
            amount = jnp.where(src_plane == first_plane + j, weight, 0.0)
            return new + src_hot[rows, :] * amount
        return extra

    def sample(field, n):
        x = field[8:16, YS, :].reshape(256, 128)
        g = dot(pick[...], jnp.concatenate(split(x, 3), axis=1))
        hot3 = jnp.concatenate([lane_hot[...]] * 3, axis=1)
        values = lax.dot_general(jnp.ones((8, 384), BF16), (g * hot3).astype(BF16), NT, preferred_element_type=F32)
        for part in range(2):
            tr[2 * n + part:2 * n + part + 1, :] = values[0:1, 128 * part:128 * part + 128]

    tr[8:16] = jnp.zeros((8, 128), F32)
    left, right = inside(-1), inside(1)

    def kappa_of(values, valid):
        value = (values.astype(F32) + MID) * COURANT
        return value * value * valid

    def fill(now, from_left, from_right):
        now[0:8, YS, :] = from_left.astype(F32) * left
        now[16:24, YS, :] = from_right.astype(F32) * right

    fields = ((u0, wa0), (u1, wa1))
    copies = [None, None]

    def round_of(r, f):
        now, old = fields[f]
        if r == 0:
            for copy in first[f]:
                copy.wait_recv()
            fill(now, rc[0, f], rc[1, f])
            old[4:8, YS, :] = rp[0, f].astype(F32) * left
            old[16:20, YS, :] = rp[1, f].astype(F32) * right
            if f == 0:
                kap[12:16] = kappa_of(rn[0], left)
                kap[24:28] = kappa_of(rn[1], right)
        else:
            for copy in copies[f]:
                copy.wait_recv()
            fill(now, rb[r - 1, f, 0], rb[r - 1, f, 1])
        n = 2 * r
        z_pass(now, 4, 16)
        advance(now, old, 4, 16, 12, plain if f else forward_extra(n))
        if f == 0:
            lap[n] = zs[4:12]
        z_pass(old, 8, 8)
        advance(old, now, 8, 8, 16, plain if f else forward_extra(n + 1))
        if f == 0:
            lap[n + 1] = zs[0:8]
        if r < 2:
            sb[r, f] = now[8:16, YS, :].astype(BF16)
            copies[f] = [
                send(sb.at[r, f], rb.at[r, f, side], round_s.at[2 * r + f, side], round_r.at[2 * r + f, side],
                     s, slab_at(step))
                for side, step in ((0, 1), (1, -1))]
            sent.extend(copies[f])
        if f == 0:
            sample(old, n)
            sample(now, n + 1)
        else:
            hom[STEPS - 1 - n] = old[8:16, YS, :]
            hom[STEPS - 2 - n] = now[8:16, YS, :]

    round_of(0, 0)
    pl.semaphore_wait(token_slab2, 2)
    tell(token_slab4, [(s, slab_at(-4)), (s, slab_at(4))])
    pl.semaphore_wait(token_z, 2)
    tell(token_core, [(core_twin, b)])
    pltpu.make_async_copy(vp, vp, vp_r).wait()
    for k in range(1, 8):
        send(vp, rv.at[k - 1], rv_s, rv_r, z_at(k), b)
    round_of(0, 1)
    round_of(1, 0)
    pl.semaphore_wait(token_slab4, 2)
    pl.semaphore_wait(token_core, 1)
    tell(token_half, [(shot_at(16), b)])
    for k in range(1, slabs):
        send(tr.at[0:8], rt.at[k - 1], tr_s, tr_r, s, slab_at(k))
    round_of(1, 1)
    round_of(2, 0)
    pl.semaphore_wait(token_half, 1)
    tell(token_beside, [(s, slab_at(-1)), (s, slab_at(1))])

    for k in range(1, slabs):
        send(tr.at[8:16], rl.at[k - 1], rl_s, rl_r, s, slab_at(k))
    round_of(2, 1)
    image = hom[0] * lap[0]
    for n in range(1, STEPS):
        image = image + hom[n] * lap[n]
    img[...] = image
    pltpu.make_async_copy(rv, rv, rv_r).wait()
    near_far = ((0, inside(-2)), (8, left), (24, right), (32, inside(2)))
    for k in range(8):
        plane = lax.rem(zi - k + 8, 8)
        for slot, (base, valid) in enumerate(near_far):
            kap[base + plane] = kappa_of(rv[k - 1, slot] if k else vp[slot], valid)
    pltpu.make_async_copy(rt, rt, tr_r).wait()
    pltpu.make_async_copy(rl, rl, rl_r).wait()
    early, late = tr[0:8], tr[8:16]
    for k in range(slabs - 1):
        early = early + rt[k]
        late = late + rl[k]
    mf[...] = jnp.zeros((8, 256), F32)
    for n in range(STEPS):
        total, at = (early, 2 * n) if n < 4 else (late, 2 * n - 8)
        trace = jnp.concatenate([total[at:at + 1], total[at + 1:at + 2]], axis=1) - obs[n]
        mis[n] = trace
        mf[n:n + 1, :] = trace
    amounts = jnp.zeros((256, 8), F32)
    for part in split(mf[...], 3):
        amounts = amounts + lax.dot_general(eye, part, NT, preferred_element_type=F32)

    def inject(n, plane, planes):
        parts = split(amounts[:, n:n + 1] * lane_hot[...], 2)
        rhs = jnp.concatenate(parts, axis=1)
        for c in range(planes // 8):
            start = (plane + 8 * c) * ROWS
            both = dot(hot[start:start + 256, :], rhs)
            yield c, (both[:, 0:128] + both[:, 128:256]).reshape(8, ROWS, 128)

    for c, values in inject(5, 0, 48):
        da[8 * c:8 * c + 8, YS, :] = values
    img[...] += da[20:28, YS, :] * lap[5]

    def with_misfit(i, j, rows, new, acc):
        return new + js[i, rows, :]

    near, old = da, db
    for n in range(4, -1, -1):
        reach = 4 * n
        lo, planes = 20 - reach, 8 + 2 * reach
        z_pass(near, lo, planes)
        for c, values in inject(n, lo, planes):
            js[8 * c:8 * c + 8] = values
        advance(near, old, lo, planes, lo - 4, with_misfit)
        near, old = old, near
        img[...] += near[20:28, YS, :] * lap[n]

    by_row = jnp.swapaxes(img[...], 0, 1).reshape(8, 2, 16, 128)
    for core in range(2):
        imgt[core] = by_row[:, core]
    core = lax.rem(s, 2)
    chip = lax.div(s, 2)
    chips = shots // 2
    swap = send(imgt.at[1 - core], ip, ip_s, ip_r, core_twin, b)
    sent.append(swap)
    swap.wait_recv()
    chip_sum[...] = imgt[core] + ip[...]
    for k in range(1, chips):
        target = lax.rem(chip + k, chips)
        send(chip_sum.at[lax.rem(target, 8)], ri.at[chip], im_s, im_r, 2 * target + core, b)
    ri[chip] = chip_sum[zi]
    row_of = lax.broadcasted_iota(jnp.int32, (8, ROWS, 128), 1)
    own_velocity = jnp.concatenate(
        [jnp.sum(jnp.where(row_of == 2 * pair + y, vel[...], 0.0), axis=1) for y in range(2)], axis=0)
    pl.semaphore_wait(token_beside, 2)
    pltpu.make_async_copy(ri.at[0:chips - 1], ri.at[0:chips - 1], im_r).wait()
    summed = ri[0]
    for k in range(1, chips):
        summed = summed + ri[k]
    update = RATE * (summed / shots)
    moved = own_velocity - update
    centered = moved - CENTER
    for y in range(2):
        fs[y] = jnp.concatenate([centered[8 * y:8 * y + 8], update[8 * y:8 * y + 8]], axis=0).astype(BF16)
    for side, first_plane in ((0, 4), (1, 0)):
        fe[side] = jnp.concatenate(
            [v[8 * y + first_plane:8 * y + first_plane + 4] for y in range(2) for v in (centered, update)],
            axis=0).astype(BF16)

    around = (-2, -1, 1, 2)
    for slot, dr in enumerate(around):
        send(fs, rf.at[slot], ft_s, ft_r, half + lax.rem(pair - dr + 16, 16), b)
    for side, dx in ((0, -1), (1, 1)):
        for dr in range(-2, 3):
            send(fe.at[side], re.at[side, dr + 2], fe_s, fe_r, half + lax.rem(pair - dr + 16, 16), slab_at(-dx))
    pltpu.make_async_copy(rf, rf, ft_r).wait()
    pltpu.make_async_copy(re, re, fe_r).wait()
    lane32 = iota(32, 128, 1)

    def row_inside(k):
        return jnp.where((2 * pair + k >= 0) & (2 * pair + k < ROWS), 1.0, 0.0).astype(F32)

    for dr in range(-2, 3):
        valid = row_inside(2 * dr)
        beside = [re[side, dr + 2].astype(F32) * (valid * (left, right)[side]) for side in range(2)]
        for y in range(2):
            own = fs[y].astype(F32) if dr == 0 else rf[around.index(dr), y].astype(F32) * valid
            values = jnp.concatenate([beside[0][8 * y:8 * y + 8], own, beside[1][8 * y:8 * y + 8]], axis=0)
            at = 2 * dr + 4 + y
            feat[0, at] = jnp.where(lane32 == 0, 0.0, pltpu.roll(values, 1, 1)).astype(BF16)
            feat[1, at] = values.astype(BF16)
            feat[2, at] = jnp.where(lane32 == 127, 0.0, pltpu.roll(values, 127, 1)).astype(BF16)

    def first_conv(i, carry):
        rhs = [
            jnp.concatenate([feat[k, pl.ds(2 * i + at + 1, 3)].reshape(96, 128) for at in range(2)], axis=1)
            for k in range(3)]
        for part in range(3):
            rows = slice(256 * part, 256 * part + 256)
            g = dot(band1[0, rows], rhs[0]) + dot(band1[1, rows], rhs[1]) + dot(band1[2, rows], rhs[2])
            for at in range(2):
                row_ok = row_inside(2 * i + at - 2)
                for x in range(4):
                    plane = b * 8 + 4 * part + x - 2
                    ok = jnp.where((plane >= 0) & (plane < slabs * 8), row_ok, 0.0)
                    value = jnp.maximum(g[64 * x:64 * x + 64, 128 * at:128 * at + 128] + b1, 0.0) * ok
                    h1[2 * i + at, 4 * part + x] = value.astype(BF16)
        return carry

    lax.fori_loop(0, 3, first_conv, 0)

    def second_conv(y, carry):
        row_ok = row_inside(y - 1)
        for x0 in range(0, 10, 2):
            halves = []
            for x in (x0, x0 + 1):
                halves.append(jnp.concatenate([h1[y + j, x:x + 3].reshape(192, 128) for j in range(3)], axis=0))
            g = dot(wm[...], jnp.concatenate(halves, axis=1))
            for half in range(2):
                x = x0 + half
                plane = b * 8 + x - 1
                ok = jnp.where((plane >= 0) & (plane < slabs * 8), row_ok, 0.0)
                value = jnp.maximum(z_combine(g[:, 128 * half:128 * half + 128], lane) + b2, 0.0) * ok
                h2[y, x] = value.astype(BF16)
        return carry

    lax.fori_loop(0, 4, second_conv, 0)

    lane1 = lax.broadcasted_iota(jnp.int32, (1, 128), 1)
    for y in range(2):
        for x in range(0, 8, 2):
            halves = []
            for at in (x, x + 1):
                halves.append(jnp.concatenate([h2[y + j, at:at + 3].reshape(192, 128) for j in range(3)], axis=0))
            pair_g = dot(w3[...], jnp.concatenate(halves, axis=1))
            for at in range(2):
                g = pair_g[0:8, 128 * at:128 * at + 128]
                low = jnp.where(lane1 == 0, 0.0, pltpu.roll(g, 1, 1)[0:1])
                high = jnp.where(lane1 == 127, 0.0, pltpu.roll(g, 127, 1)[2:3])
                i = 8 * y + x + at
                row[i:i + 1, :] = moved[i:i + 1] + (g[1:2] + low + high + b3[0])

    for k in range(1, 16):
        send(row, ro.at[k - 1], ou_s, ou_r, half + lax.rem(pair + k, 16), b)
    by_owner[pair] = row[...]
    pltpu.make_async_copy(ro, ro, ou_r).wait()
    for k in range(1, 16):
        by_owner[lax.rem(pair - k + 16, 16)] = ro[k - 1]
    out[...] = jnp.swapaxes(by_owner[...].reshape(ROWS, 8, 128), 0, 1)

    for copy in sent:
        copy.wait_send()
    pltpu.make_async_copy(vp, vp, vp_s).wait()
    pltpu.make_async_copy(rv, rv, rv_s).wait()
    pltpu.make_async_copy(rt, rt, tr_s).wait()
    pltpu.make_async_copy(rl, rl, rl_s).wait()
    pltpu.make_async_copy(ri.at[0:chips - 1], ri.at[0:chips - 1], im_s).wait()
    pltpu.make_async_copy(rf, rf, ft_s).wait()
    pltpu.make_async_copy(re, re, fe_s).wait()
    pltpu.make_async_copy(ro, ro, ou_s).wait()


def shards(slabs, shots, previous_field, current_field, adjoint_next, adjoint_current, velocity, wavelet, source_cell,
           receiver_cell, observed, weight_in, bias_in, weight_mid, bias_mid, weight_out, bias_out):
    vmem = pl.BlockSpec(memory_space=pltpu.VMEM)
    smem = pl.BlockSpec(memory_space=pltpu.SMEM)
    f32 = lambda *shape: pltpu.VMEM(shape, F32)
    bf = lambda *shape: pltpu.VMEM(shape, BF16)
    dma = pltpu.SemaphoreType.DMA
    arrays = (previous_field, current_field, adjoint_next, adjoint_current, velocity, receiver_cell,
              jnp.swapaxes(observed, 0, 1), weight_in, bias_in[None], weight_mid, bias_mid[None], weight_out.reshape(27, 64))
    scratch = [pltpu.VMEM(a.shape, a.dtype) for a in arrays] + [
        f32(24, 48, 128), f32(24, 48, 128), f32(24, 48, 128), f32(24, 48, 128),
        f32(48, 48, 128), f32(48, 48, 128), f32(40, 32, 128), f32(40, 32, 128), f32(40, 32, 128),
        f32(6, 8, 32, 128), f32(6, 8, 32, 128), f32(8, 32, 128), f32(2, 8, 16, 128), f32(8, 16, 128), f32(8, 16, 128),
        bf(8, 32, 128), bf(4, 32, 128), bf(7, 4, 32, 128), bf(2, 4, 32, 128), bf(2, 2, 8, 32, 128), bf(2, 2, 4, 32, 128),
        bf(2, 2, 8, 32, 128), bf(2, 2, 2, 8, 32, 128),
        f32(16, 128), f32(slabs - 1, 8, 128), f32(slabs - 1, 8, 128), f32(8, 256),
        bf(1536, 256), bf(256, 256), f32(256, 128), f32(32, 128), bf(256, 128), bf(128, 128),
        f32(shots // 2, 16, 128), bf(2, 16, 128), bf(2, 16, 128), bf(4, 2, 16, 128), bf(2, 5, 16, 128), bf(3, 10, 32, 128),
        f32(96, 64), bf(192, 32), bf(192, 576), bf(16, 576), bf(3, 768, 96),
        bf(6, 12, 64, 128), bf(4, 10, 64, 128), f32(16, 128), f32(15, 16, 128), f32(16, 16, 128),
        dma((2, 5)), dma((2, 5)), dma, dma, dma, dma, dma((4, 2)), dma((4, 2)),
    ] + [dma] * 8 + [dma((12,))] + [dma] * 6 + [pltpu.SemaphoreType.REGULAR] * 6
    rows, misfit = pl.pallas_call(
        functools.partial(kernel, slabs, shots),
        out_shape=(jax.ShapeDtypeStruct(velocity.shape, F32), jax.ShapeDtypeStruct((STEPS, 1, 256), F32)),
        in_specs=[smem, smem, smem] + [pl.BlockSpec(memory_space=pl.ANY)] * 12,
        out_specs=(vmem, vmem),
        scratch_shapes=scratch,
        compiler_params=pltpu.CompilerParams(
            collective_id=0, has_side_effects=True, vmem_limit_bytes=60 * 1024 * 1024),
    )(wavelet, source_cell, bias_out, *arrays)
    return rows, jnp.swapaxes(misfit, 0, 1)


def solution(mesh):
    placed = (
        P("shot", "slab", None, None), P("shot", "slab", None, None), P("shot", "slab", None, None),
        P("shot", "slab", None, None), P("slab", None, None), P("shot", None), P("shot"), P("shot", None),
        P("shot", None, None), P(), P(), P(), P(), P(), P(),
    )
    return jax.shard_map(
        functools.partial(shards, mesh.shape["slab"], mesh.shape["shot"]),
        mesh=mesh,
        in_specs=placed,
        out_specs=(P("slab", None, None), P("shot", None, None)),
        check_vma=False,
    )
```

```python
import functools

import jax
import jax.numpy as jnp
from jax import lax
from jax.experimental import pallas as pl
from jax.experimental.pallas import tpu as pltpu
from jax.sharding import PartitionSpec as P

COEFFS = (-205.0 / 72.0, 8.0 / 5.0, -1.0 / 5.0, 8.0 / 315.0, -1.0 / 560.0)
COURANT = 0.1
RATE = 0.2
CENTER = 3.0
MID = 2.75
MESH = pl.DeviceIdType.MESH
F32 = jnp.float32
BF16 = jnp.bfloat16
NT = (((1,), (1,)), ((), ()))
STEPS = 6
TOP, ROWS = 8, 32
YS = slice(TOP, TOP + ROWS)


def dot(a, b):
    return jnp.dot(a, b, preferred_element_type=F32)


def split(x, pieces):
    parts = []
    for _ in range(pieces):
        part = x.astype(BF16)
        parts.append(part)
        x = x - part.astype(F32)
    return parts


def z_combine(g, lane):
    low = jnp.where(lane == 0, 0.0, pltpu.roll(g[0:64], 1, 1))
    high = jnp.where(lane == 127, 0.0, pltpu.roll(g[128:192], 127, 1))
    return g[64:128] + low + high


def kernel(
    slabs, shots,
    wav, src, b3, *refs,
):
    hbm, (out, mis), loaded, rest = refs[:12], refs[12:14], refs[14:26], refs[26:]
    prev, cur, anext, acur, vel, rec, obs, wi, bi, wd, bd, wo = loaded
    (
        u0, u1, wa0, wa1, da, db, zs, js, kap, lap, hom, img, imgt, ip, chip_sum, sv, vp, rv, rn, rc, rp, sb, rb, tr, rt, rl, mf, hot, pick, lane_hot, src_hot, bands, bandl, ri, fs, fe, rf, re, feat, wf, w1, wm, w3, band1, h1, h2, taps, row, ro, by_owner, init_s, init_r, vp_s, vp_r, rv_s, rv_r, round_s, round_r, tr_s, tr_r, im_s, im_r, ft_s, ft_r, ou_s, ou_r, load_s, ip_s, ip_r, rl_s, rl_r, fe_s, fe_r,
        token_slab2, token_slab4, token_z, token_core, token_half, token_beside,
    ) = rest
    s = lax.axis_index("shot")
    b = lax.axis_index("slab")

    def shot_at(k):
        return lax.rem(s + k + shots, shots)

    def slab_at(k):
        return lax.rem(b + k + slabs, slabs)

    def inside(k):
        return jnp.where((b + k >= 0) & (b + k < slabs), 1.0, 0.0).astype(F32)

    def send(source, target, ss, rs, shot, slab):
        copy = pltpu.make_async_remote_copy(
            src_ref=source, dst_ref=target, send_sem=ss, recv_sem=rs,
            device_id=(shot, slab), device_id_type=MESH)
        copy.start()
        return copy

    barrier = pltpu.get_barrier_semaphore()
    zi = lax.rem(lax.div(s, 2), 8)
    pair = lax.rem(s, 16)
    half = s - pair

    def z_at(k):
        return s + 2 * (lax.rem(zi + k + 8, 8) - zi)

    core_twin = s + 1 - 2 * lax.rem(s, 2)
    peers = [(s, slab_at(k)) for k in (-2, -1, 1, 2)] + [(z_at(k), b) for k in (-2, -1, 1, 2)]
    peers += [(core_twin, b), (shot_at(16), b)]

    def tell(token, others):
        for other in others:
            pl.semaphore_signal(token, inc=1, device_id=other, device_id_type=MESH)

    for peer in peers:
        pl.semaphore_signal(barrier, inc=1, device_id=peer, device_id_type=MESH)

    loads = [pltpu.make_async_copy(hbm[at], loaded[at], load_s.at[at]) for at in range(12)]
    for at in (4, 1, 0, 3, 2, 5, 6, 7, 8, 9, 10, 11):
        loads[at].start()
    pl.semaphore_wait(barrier, len(peers))
    tell(token_slab2, [(s, slab_at(-2)), (s, slab_at(2))])
    tell(token_z, [(z_at(-2), b), (z_at(2), b)])

    sent = []
    first = ([], [])

    def send_first(f):
        now, old = ((hbm[1], hbm[0]), (acur, anext))[f]
        for side, step in ((0, 1), (1, -1)):
            target = slab_at(step)
            edge = pl.ds(4, 4) if step == 1 else pl.ds(0, 4)
            at = init_s.at[side, 2 * f], init_r.at[side, 2 * f]
            first[f].append(send(now.at[0], rc.at[side, f], *at, s, target))
            at = init_s.at[side, 2 * f + 1], init_r.at[side, 2 * f + 1]
            first[f].append(send(old.at[0, edge], rp.at[side, f], *at, s, target))
        for side, step in ((0, 1), (1, -1)) if f == 0 else ():
            if side == 0:
                loads[4].wait()
                sv[...] = (vel[...] - MID).astype(BF16)
            edge = pl.ds(4, 4) if step == 1 else pl.ds(0, 4)
            first[f].append(send(sv.at[edge], rn.at[side], init_s.at[side, 4], init_r.at[side, 4], s, slab_at(step)))

    send_first(0)

    for at in (0, 1, 2, 3, *range(5, 12)):
        loads[at].wait()
    lane = lax.broadcasted_iota(jnp.int32, (64, 128), 1)
    diff = jnp.abs(lax.broadcasted_iota(jnp.int32, (128, 128), 0) - lax.broadcasted_iota(jnp.int32, (128, 128), 1))
    band = jnp.where(diff == 0, 3.0 * COEFFS[0], 0.0)
    for m in range(1, 5):
        band = jnp.where(diff == m, COEFFS[m], band)
    band_h, band_l = split(band, 2)
    bands[0:128, :] = band_h
    bands[128:256, :] = band_h
    bandl[...] = band_l

    for ref in (u0, u1, wa0, wa1, da, db):
        ref[:, 0:TOP, :] = jnp.zeros((ref.shape[0], TOP, 128), F32)
        ref[:, TOP + ROWS:, :] = jnp.zeros((ref.shape[0], 8, 128), F32)
    db[:, YS, :] = jnp.zeros((db.shape[0], ROWS, 128), F32)
    u0[8:16, YS, :] = cur[0].astype(F32)
    u1[8:16, YS, :] = acur[0].astype(F32)
    wa0[8:16, YS, :] = prev[0].astype(F32)
    wa1[8:16, YS, :] = anext[0].astype(F32)
    scaled = vel[...] * COURANT
    kap[16:24] = scaled * scaled

    cells = rec[...]
    rec_row = lax.shift_right_logical(cells, 7)
    rec_lane = cells & 127
    sub = lax.broadcasted_iota(jnp.int32, (8, 256), 0)
    digits = jnp.where(sub == 0, lax.shift_right_logical(rec_row, 6),
                       jnp.where(sub == 1, rec_row & 63, jnp.where(sub == 2, rec_lane, 0)))
    eye = jnp.where(
        lax.broadcasted_iota(jnp.int32, (256, 256), 0) == lax.broadcasted_iota(jnp.int32, (256, 256), 1),
        1.0, 0.0).astype(BF16)
    columns = lax.dot_general(eye, digits.astype(F32).astype(BF16), NT, preferred_element_type=F32)
    row_col = columns[:, 0:1] * 64.0 + columns[:, 1:2] - (b * 256).astype(F32)
    lane_col = columns[:, 2:3]
    lane_hot[...] = jnp.where(lane_col == lax.broadcasted_iota(jnp.int32, (256, 128), 1).astype(F32), 1.0, 0.0)
    pick[...] = jnp.where(
        row_col == lax.broadcasted_iota(jnp.int32, (256, 256), 1).astype(F32), 1.0, 0.0).astype(BF16)
    relative = rec_row - (b * 256 - 20 * ROWS)
    for q in range(6):
        hot[256 * q:256 * q + 256, :] = jnp.where(
            lax.broadcasted_iota(jnp.int32, (256, 256), 0) + 256 * q == relative, 1.0, 0.0).astype(BF16)
    cell = src[0]
    src_plane = lax.shift_right_logical(cell, 12)
    src_row = lax.shift_right_logical(cell, 7) & 31
    src_lane = cell & 127
    src_hot[...] = jnp.where(
        (lax.broadcasted_iota(jnp.int32, (ROWS, 128), 0) == src_row)
        & (lax.broadcasted_iota(jnp.int32, (ROWS, 128), 1) == src_lane), 1.0, 0.0)

    def iota(rows, columns, axis):
        return lax.broadcasted_iota(jnp.int32, (rows, columns), axis)

    def one_hot(condition):
        return jnp.where(condition, 1.0, 0.0).astype(BF16)

    eye64 = one_hot(iota(64, 64, 0) == iota(64, 64, 1))
    wf[...] = jnp.zeros((96, 64), F32)
    for t in range(27):
        wf[2 * t:2 * t + 2, :] = wi[t].astype(F32)
    wf[64:91, :] = wo[...].astype(F32)
    taps_in = wf[0:64, :].astype(BF16)
    taps_out = wf[64:96, :].astype(BF16)
    q = iota(96, 64, 0)
    i, j, c = (q >> 3) & 3, (q >> 1) & 3, q & 1
    wanted = one_hot((iota(96, 64, 1) == (9 * i + 3 * j + (q >> 5)) * 2 + c) & (i < 3) & (j < 3))
    chosen = dot(wanted, taps_in).astype(BF16)
    for k in range(3):
        w1[64 * k:64 * k + 64, :] = lax.dot_general(
            eye64, chosen[32 * k:32 * k + 32], NT, preferred_element_type=F32).astype(BF16)
    for k in range(3):
        for u in range(0, 9, 2):
            blocks = [wd[9 * (v % 3) + 3 * (v // 3) + k] for v in range(u, min(u + 2, 9))]
            both = lax.dot_general(eye64, jnp.concatenate(blocks, axis=0), NT, preferred_element_type=F32)
            wm[64 * k:64 * k + 64, 64 * u:64 * (u + len(blocks))] = both.astype(BF16)
    u, k = iota(80, 32, 0) >> 3, iota(80, 32, 0) & 7
    j = jnp.where(u >= 3, 1, 0) + jnp.where(u >= 6, 1, 0)
    wanted = one_hot((iota(80, 32, 1) == 9 * (u - 3 * j) + 3 * j + k) & (k < 3) & (u < 9))
    w3[...] = dot(wanted, taps_out).astype(BF16)
    sub64 = iota(8, 64, 0)
    biases = jnp.zeros((8, 64), F32)
    for at, part in enumerate(split(bi[...], 3) + split(bd[...], 3)):
        biases = jnp.where(sub64 == at, part.astype(F32), biases)
    bias_col = lax.dot_general(eye64, biases.astype(BF16), NT, preferred_element_type=F32)
    b1 = bias_col[:, 0:1] + bias_col[:, 1:2] + bias_col[:, 2:3]
    b2 = bias_col[:, 3:4] + bias_col[:, 4:5] + bias_col[:, 5:6]
    r, col = iota(32, 96, 0), iota(32, 96, 1)
    group = jnp.where(col >= 32, 1, 0) + jnp.where(col >= 64, 1, 0)
    rest = col - 32 * group
    before, after = rest < 8, rest >= 24
    edge_rest = jnp.where(after, rest - 24, rest)
    channel = jnp.where(before | after, edge_rest >> 2, (rest - 8) >> 3)
    plane_of = jnp.where(before, edge_rest & 3, jnp.where(after, 12 + (edge_rest & 3), 4 + ((rest - 8) & 7)))
    fits = (((r >> 1) & 3) == group) & ((r & 1) == channel) & ((r >> 3) < 3)
    shift = plane_of - (r >> 3) - 1
    for x in range(12):
        wide = dot(w1[...], one_hot(fits & (shift == x))).astype(BF16)
        for k in range(3):
            band1[k, 64 * x:64 * x + 64, :] = wide[64 * k:64 * k + 64]

    send_first(1)
    for slot, step in enumerate((2, 1, -1, -2)):
        send(sv.at[zi], vp.at[slot], vp_s, vp_r, s, slab_at(step))
    sent += first[0] + first[1]

    def z_pass(field, lo, n):
        for c in range(n // 8):
            x = field[lo + 8 * c:lo + 8 * c + 8, YS, :].reshape(256, 128)
            hi, low = split(x, 2)
            z = dot(jnp.concatenate([hi, low], axis=1), bands[...]) + dot(hi, bandl[...])
            zs[8 * c:8 * c + 8] = z.reshape(8, ROWS, 128)

    def advance(field, old, lo, n, kap_lo, extra):
        def four(g, carry):
            i0 = 4 * g
            j0 = lo + i0
            for q in range(ROWS // 8):
                rows = slice(8 * q, 8 * q + 8)
                window = [field[j0 + k - 4, TOP + 8 * q:TOP + 8 * q + 8, :] for k in range(12)]
                for p in range(4):
                    acc = zs[i0 + p, rows, :]
                    for m in range(1, 5):
                        at = TOP + 8 * q
                        around = (window[p + 4 + m] + window[p + 4 - m]) + (
                            field[j0 + p, at + m:at + m + 8, :] + field[j0 + p, at - m:at - m + 8, :])
                        acc = acc + COEFFS[m] * around
                    ys = slice(TOP + 8 * q, TOP + 8 * q + 8)
                    new = 2.0 * window[p + 4] - old[j0 + p, ys, :] + kap[kap_lo + i0 + p, rows, :] * acc
                    old[j0 + p, ys, :] = extra(i0 + p, j0 + p, rows, new, acc)
            return carry
        lax.fori_loop(0, n // 4, four, 0)

    def plain(i, j, rows, new, acc):
        return new

    def forward_extra(n):
        weight = wav[0, n]
        first_plane = b * 8 - 8

        def extra(i, j, rows, new, acc):
            zs[i, rows, :] = acc
            amount = jnp.where(src_plane == first_plane + j, weight, 0.0)
            return new + src_hot[rows, :] * amount
        return extra

    def sample(field, n):
        x = field[8:16, YS, :].reshape(256, 128)
        g = dot(pick[...], jnp.concatenate(split(x, 3), axis=1))
        hot3 = jnp.concatenate([lane_hot[...]] * 3, axis=1)
        values = lax.dot_general(jnp.ones((8, 384), BF16), (g * hot3).astype(BF16), NT, preferred_element_type=F32)
        for part in range(2):
            tr[2 * n + part:2 * n + part + 1, :] = values[0:1, 128 * part:128 * part + 128]

    tr[8:16] = jnp.zeros((8, 128), F32)
    left, right = inside(-1), inside(1)

    def kappa_of(values, valid):
        value = (values.astype(F32) + MID) * COURANT
        return value * value * valid

    def fill(now, from_left, from_right):
        now[0:8, YS, :] = from_left.astype(F32) * left
        now[16:24, YS, :] = from_right.astype(F32) * right

    fields = ((u0, wa0), (u1, wa1))
    copies = [None, None]

    def round_of(r, f):
        now, old = fields[f]
        if r == 0:
            for copy in first[f]:
                copy.wait_recv()
            fill(now, rc[0, f], rc[1, f])
            old[4:8, YS, :] = rp[0, f].astype(F32) * left
            old[16:20, YS, :] = rp[1, f].astype(F32) * right
            if f == 0:
                kap[12:16] = kappa_of(rn[0], left)
                kap[24:28] = kappa_of(rn[1], right)
        else:
            for copy in copies[f]:
                copy.wait_recv()
            fill(now, rb[r - 1, f, 0], rb[r - 1, f, 1])
        n = 2 * r
        z_pass(now, 4, 16)
        advance(now, old, 4, 16, 12, plain if f else forward_extra(n))
        if f == 0:
            lap[n] = zs[4:12]
        z_pass(old, 8, 8)
        advance(old, now, 8, 8, 16, plain if f else forward_extra(n + 1))
        if f == 0:
            lap[n + 1] = zs[0:8]
        if r < 2:
            sb[r, f] = now[8:16, YS, :].astype(BF16)
            copies[f] = [
                send(sb.at[r, f], rb.at[r, f, side], round_s.at[2 * r + f, side], round_r.at[2 * r + f, side],
                     s, slab_at(step))
                for side, step in ((0, 1), (1, -1))]
            sent.extend(copies[f])
        if f == 0:
            sample(old, n)
            sample(now, n + 1)
        else:
            hom[STEPS - 1 - n] = old[8:16, YS, :]
            hom[STEPS - 2 - n] = now[8:16, YS, :]

    round_of(0, 0)
    pl.semaphore_wait(token_slab2, 2)
    tell(token_slab4, [(s, slab_at(-4)), (s, slab_at(4))])
    pl.semaphore_wait(token_z, 2)
    tell(token_core, [(core_twin, b)])
    pltpu.make_async_copy(vp, vp, vp_r).wait()
    for k in range(1, 8):
        send(vp, rv.at[k - 1], rv_s, rv_r, z_at(k), b)
    round_of(0, 1)
    round_of(1, 0)
    pl.semaphore_wait(token_slab4, 2)
    pl.semaphore_wait(token_core, 1)
    tell(token_half, [(shot_at(16), b)])
    for k in range(1, slabs):
        send(tr.at[0:8], rt.at[k - 1], tr_s, tr_r, s, slab_at(k))
    round_of(1, 1)
    round_of(2, 0)
    pl.semaphore_wait(token_half, 1)
    tell(token_beside, [(s, slab_at(-1)), (s, slab_at(1))])

    for k in range(1, slabs):
        send(tr.at[8:16], rl.at[k - 1], rl_s, rl_r, s, slab_at(k))
    pltpu.make_async_copy(rv, rv, rv_r).wait()
    near_far = ((0, inside(-2)), (8, left), (24, right), (32, inside(2)))
    for k in range(8):
        plane = lax.rem(zi - k + 8, 8)
        for slot, (base, valid) in enumerate(near_far):
            kap[base + plane] = kappa_of(rv[k - 1, slot] if k else vp[slot], valid)
    round_of(2, 1)
    image = hom[0] * lap[0]
    for n in range(1, STEPS):
        image = image + hom[n] * lap[n]
    img[...] = image
    pltpu.make_async_copy(rt, rt, tr_r).wait()
    pltpu.make_async_copy(rl, rl, rl_r).wait()
    early, late = tr[0:8], tr[8:16]
    for k in range(slabs - 1):
        early = early + rt[k]
        late = late + rl[k]
    mf[...] = jnp.zeros((8, 256), F32)
    for n in range(STEPS):
        total, at = (early, 2 * n) if n < 4 else (late, 2 * n - 8)
        trace = jnp.concatenate([total[at:at + 1], total[at + 1:at + 2]], axis=1) - obs[n]
        mis[n] = trace
        mf[n:n + 1, :] = trace
    amounts = jnp.zeros((256, 8), F32)
    for part in split(mf[...], 3):
        amounts = amounts + lax.dot_general(eye, part, NT, preferred_element_type=F32)

    def inject(n, plane, planes):
        parts = split(amounts[:, n:n + 1] * lane_hot[...], 2)
        rhs = jnp.concatenate(parts, axis=1)
        for c in range(planes // 8):
            start = (plane + 8 * c) * ROWS
            both = dot(hot[start:start + 256, :], rhs)
            yield c, (both[:, 0:128] + both[:, 128:256]).reshape(8, ROWS, 128)

    for c, values in inject(5, 0, 48):
        da[8 * c:8 * c + 8, YS, :] = values
    img[...] += da[20:28, YS, :] * lap[5]

    def with_misfit(i, j, rows, new, acc):
        return new + js[i, rows, :]

    near, old = da, db
    for n in range(4, -1, -1):
        reach = 4 * n
        lo, planes = 20 - reach, 8 + 2 * reach
        z_pass(near, lo, planes)
        for c, values in inject(n, lo, planes):
            js[8 * c:8 * c + 8] = values
        advance(near, old, lo, planes, lo - 4, with_misfit)
        near, old = old, near
        img[...] += near[20:28, YS, :] * lap[n]

    by_row = jnp.swapaxes(img[...], 0, 1).reshape(8, 2, 16, 128)
    for core in range(2):
        imgt[core] = by_row[:, core]
    core = lax.rem(s, 2)
    chip = lax.div(s, 2)
    chips = shots // 2
    swap = send(imgt.at[1 - core], ip, ip_s, ip_r, core_twin, b)
    sent.append(swap)
    swap.wait_recv()
    chip_sum[...] = imgt[core] + ip[...]
    for k in range(1, chips):
        target = lax.rem(chip + k, chips)
        send(chip_sum.at[lax.rem(target, 8)], ri.at[chip], im_s, im_r, 2 * target + core, b)
    ri[chip] = chip_sum[zi]
    row_of = lax.broadcasted_iota(jnp.int32, (8, ROWS, 128), 1)
    own_velocity = jnp.concatenate(
        [jnp.sum(jnp.where(row_of == 2 * pair + y, vel[...], 0.0), axis=1) for y in range(2)], axis=0)
    pl.semaphore_wait(token_beside, 2)
    pltpu.make_async_copy(ri.at[0:chips - 1], ri.at[0:chips - 1], im_r).wait()
    summed = ri[0]
    for k in range(1, chips):
        summed = summed + ri[k]
    update = RATE * (summed / shots)
    moved = own_velocity - update
    centered = moved - CENTER
    for y in range(2):
        fs[y] = jnp.concatenate([centered[8 * y:8 * y + 8], update[8 * y:8 * y + 8]], axis=0).astype(BF16)
    for side, first_plane in ((0, 4), (1, 0)):
        fe[side] = jnp.concatenate(
            [v[8 * y + first_plane:8 * y + first_plane + 4] for y in range(2) for v in (centered, update)],
            axis=0).astype(BF16)

    around = (-2, -1, 1, 2)
    for slot, dr in enumerate(around):
        send(fs, rf.at[slot], ft_s, ft_r, half + lax.rem(pair - dr + 16, 16), b)
    for side, dx in ((0, -1), (1, 1)):
        for dr in range(-2, 3):
            send(fe.at[side], re.at[side, dr + 2], fe_s, fe_r, half + lax.rem(pair - dr + 16, 16), slab_at(-dx))
    pltpu.make_async_copy(rf, rf, ft_r).wait()
    pltpu.make_async_copy(re, re, fe_r).wait()
    lane32 = iota(32, 128, 1)

    def row_inside(k):
        return jnp.where((2 * pair + k >= 0) & (2 * pair + k < ROWS), 1.0, 0.0).astype(F32)

    for dr in range(-2, 3):
        valid = row_inside(2 * dr)
        beside = [re[side, dr + 2].astype(F32) * (valid * (left, right)[side]) for side in range(2)]
        for y in range(2):
            own = fs[y].astype(F32) if dr == 0 else rf[around.index(dr), y].astype(F32) * valid
            values = jnp.concatenate([beside[0][8 * y:8 * y + 8], own, beside[1][8 * y:8 * y + 8]], axis=0)
            at = 2 * dr + 4 + y
            feat[0, at] = jnp.where(lane32 == 0, 0.0, pltpu.roll(values, 1, 1)).astype(BF16)
            feat[1, at] = values.astype(BF16)
            feat[2, at] = jnp.where(lane32 == 127, 0.0, pltpu.roll(values, 127, 1)).astype(BF16)

    def first_conv(i, carry):
        rhs = [
            jnp.concatenate([feat[k, pl.ds(2 * i + at + 1, 3)].reshape(96, 128) for at in range(2)], axis=1)
            for k in range(3)]
        for part in range(3):
            rows = slice(256 * part, 256 * part + 256)
            g = dot(band1[0, rows], rhs[0]) + dot(band1[1, rows], rhs[1]) + dot(band1[2, rows], rhs[2])
            for at in range(2):
                row_ok = row_inside(2 * i + at - 2)
                for x in range(4):
                    plane = b * 8 + 4 * part + x - 2
                    ok = jnp.where((plane >= 0) & (plane < slabs * 8), row_ok, 0.0)
                    value = jnp.maximum(g[64 * x:64 * x + 64, 128 * at:128 * at + 128] + b1, 0.0) * ok
                    h1[2 * i + at, 4 * part + x] = value.astype(BF16)
        return carry

    lax.fori_loop(0, 3, first_conv, 0)

    def second_conv(y, carry):
        row_ok = row_inside(y - 1)
        for x0 in range(0, 10, 2):
            halves = []
            for x in (x0, x0 + 1):
                halves.append(jnp.concatenate([h1[y + j, x:x + 3].reshape(192, 128) for j in range(3)], axis=0))
            g = dot(wm[...], jnp.concatenate(halves, axis=1))
            for half in range(2):
                x = x0 + half
                plane = b * 8 + x - 1
                ok = jnp.where((plane >= 0) & (plane < slabs * 8), row_ok, 0.0)
                value = jnp.maximum(z_combine(g[:, 128 * half:128 * half + 128], lane) + b2, 0.0) * ok
                h2[y, x] = value.astype(BF16)
        return carry

    lax.fori_loop(0, 4, second_conv, 0)

    lane1 = lax.broadcasted_iota(jnp.int32, (1, 128), 1)
    for y in range(4):
        for x in range(0, 10, 2):
            g = dot(w3[...], jnp.concatenate([h2[y, x], h2[y, x + 1]], axis=1))
            taps[y, x] = g[0:72, 0:128]
            taps[y, x + 1] = g[0:72, 128:256]
    for y in range(2):
        for x in range(8):
            g = taps[y, x, 0:8]
            for u in range(1, 9):
                g = g + taps[y + u // 3, x + u % 3, 8 * u:8 * u + 8]
            low = jnp.where(lane1 == 0, 0.0, pltpu.roll(g, 1, 1)[0:1])
            high = jnp.where(lane1 == 127, 0.0, pltpu.roll(g, 127, 1)[2:3])
            i = 8 * y + x
            row[i:i + 1, :] = moved[i:i + 1] + (g[1:2] + low + high + b3[0])

    for k in range(1, 16):
        send(row, ro.at[k - 1], ou_s, ou_r, half + lax.rem(pair + k, 16), b)
    by_owner[pair] = row[...]
    pltpu.make_async_copy(ro, ro, ou_r).wait()
    for k in range(1, 16):
        by_owner[lax.rem(pair - k + 16, 16)] = ro[k - 1]
    out[...] = jnp.swapaxes(by_owner[...].reshape(ROWS, 8, 128), 0, 1)

    for copy in sent:
        copy.wait_send()
    pltpu.make_async_copy(vp, vp, vp_s).wait()
    pltpu.make_async_copy(rv, rv, rv_s).wait()
    pltpu.make_async_copy(rt, rt, tr_s).wait()
    pltpu.make_async_copy(rl, rl, rl_s).wait()
    pltpu.make_async_copy(ri.at[0:chips - 1], ri.at[0:chips - 1], im_s).wait()
    pltpu.make_async_copy(rf, rf, ft_s).wait()
    pltpu.make_async_copy(re, re, fe_s).wait()
    pltpu.make_async_copy(ro, ro, ou_s).wait()


def shards(slabs, shots, previous_field, current_field, adjoint_next, adjoint_current, velocity, wavelet, source_cell,
           receiver_cell, observed, weight_in, bias_in, weight_mid, bias_mid, weight_out, bias_out):
    vmem = pl.BlockSpec(memory_space=pltpu.VMEM)
    smem = pl.BlockSpec(memory_space=pltpu.SMEM)
    f32 = lambda *shape: pltpu.VMEM(shape, F32)
    bf = lambda *shape: pltpu.VMEM(shape, BF16)
    dma = pltpu.SemaphoreType.DMA
    arrays = (previous_field, current_field, adjoint_next, adjoint_current, velocity, receiver_cell,
              jnp.swapaxes(observed, 0, 1), weight_in, bias_in[None], weight_mid, bias_mid[None], weight_out.reshape(27, 64))
    scratch = [pltpu.VMEM(a.shape, a.dtype) for a in arrays] + [
        f32(24, 48, 128), f32(24, 48, 128), f32(24, 48, 128), f32(24, 48, 128),
        f32(48, 48, 128), f32(48, 48, 128), f32(40, 32, 128), f32(40, 32, 128), f32(40, 32, 128),
        f32(6, 8, 32, 128), f32(6, 8, 32, 128), f32(8, 32, 128), f32(2, 8, 16, 128), f32(8, 16, 128), f32(8, 16, 128),
        bf(8, 32, 128), bf(4, 32, 128), bf(7, 4, 32, 128), bf(2, 4, 32, 128), bf(2, 2, 8, 32, 128), bf(2, 2, 4, 32, 128),
        bf(2, 2, 8, 32, 128), bf(2, 2, 2, 8, 32, 128),
        f32(16, 128), f32(slabs - 1, 8, 128), f32(slabs - 1, 8, 128), f32(8, 256),
        bf(1536, 256), bf(256, 256), f32(256, 128), f32(32, 128), bf(256, 128), bf(128, 128),
        f32(shots // 2, 16, 128), bf(2, 16, 128), bf(2, 16, 128), bf(4, 2, 16, 128), bf(2, 5, 16, 128), bf(3, 10, 32, 128),
        f32(96, 64), bf(192, 32), bf(192, 576), bf(80, 64), bf(3, 768, 96),
        bf(6, 12, 64, 128), bf(4, 10, 64, 128), f32(4, 10, 72, 128), f32(16, 128), f32(15, 16, 128), f32(16, 16, 128),
        dma((2, 5)), dma((2, 5)), dma, dma, dma, dma, dma((4, 2)), dma((4, 2)),
    ] + [dma] * 8 + [dma((12,))] + [dma] * 6 + [pltpu.SemaphoreType.REGULAR] * 6
    rows, misfit = pl.pallas_call(
        functools.partial(kernel, slabs, shots),
        out_shape=(jax.ShapeDtypeStruct(velocity.shape, F32), jax.ShapeDtypeStruct((STEPS, 1, 256), F32)),
        in_specs=[smem, smem, smem] + [pl.BlockSpec(memory_space=pl.ANY)] * 12,
        out_specs=(vmem, vmem),
        scratch_shapes=scratch,
        compiler_params=pltpu.CompilerParams(
            collective_id=0, has_side_effects=True, vmem_limit_bytes=60 * 1024 * 1024),
    )(wavelet, source_cell, bias_out, *arrays)
    return rows, jnp.swapaxes(misfit, 0, 1)


def solution(mesh):
    placed = (
        P("shot", "slab", None, None), P("shot", "slab", None, None), P("shot", "slab", None, None),
        P("shot", "slab", None, None), P("slab", None, None), P("shot", None), P("shot"), P("shot", None),
        P("shot", None, None), P(), P(), P(), P(), P(), P(),
    )
    return jax.shard_map(
        functools.partial(shards, mesh.shape["slab"], mesh.shape["shot"]),
        mesh=mesh,
        in_specs=placed,
        out_specs=(P("slab", None, None), P("shot", None, None)),
        check_vma=False,
    )
```
